32 devices in a mesh: crop: 16 (over z, y, x), seq: 2 (over core).
Axes of the slice: x: 2, y: 2, z: 4, core: 2. Of those that a mesh axis runs over, the one named last changes fastest.
Arguments:
- single: bfloat16 [5120, 768], P(('crop', 'seq')), may hold values from -6 to 6
- conditioning: bfloat16 [5120, 384], P(('crop', 'seq')), may hold values from -6 to 6
- pair_features: bfloat16 [16, 320, 320, 128], P('crop', 'seq'), may hold values from -6 to 6
- segments: int32 [16, 320], P('crop'), may hold values from 0 to 3, never falling along the last dimension, each value on 1 to 160 neighbouring positions
- pad_mask: int32 [16, 320], P('crop'), may hold values from 0 to 1, as said below
- cotangent: bfloat16 [5120, 768], P(('crop', 'seq')), may hold values from -6 to 6
- cond_gain: bfloat16 [384, 2], replicated, may hold values from 0.099609375 to 1.8984375
- cond_weight: bfloat16 [384, 6, 768], replicated, may hold values from -0.3125 to 0.3125
- biases: bfloat16 [768, 5], replicated, may hold values from -3 to 3
- attn_weight: bfloat16 [768, 4, 768], replicated, may hold values from -0.21875 to 0.21875
- out_weight: bfloat16 [768, 768], replicated, may hold values from -1.75 to 1.75
- pair_gain: bfloat16 [128], replicated, may hold values from 0.099609375 to 1.8984375
- pair_weight: bfloat16 [128, 16], replicated, may hold values from -0.5 to 0.5
- expand_weight: bfloat16 [768, 2, 1536], replicated, may hold values from -0.21875 to 0.21875
- contract_weight: bfloat16 [1536, 768], replicated, may hold values from -0.15625 to 0.15625
Outputs:
- layer_out: bfloat16 [5120, 768], P(('crop', 'seq'))
- grad_single: float32 [5120, 768], P(('crop', 'seq'))
- grad_conditioning: float32 [5120, 384], P(('crop', 'seq'))
- grad_pair: bfloat16 [16, 320, 320, 128], P('crop', 'seq')
- grad_cond_gain: float32 [384, 2], P(('crop', 'seq'))
- grad_cond_weight: float32 [384, 6, 768], P(('crop', 'seq'))
- grad_biases: float32 [768, 5], P(('crop', 'seq'))
- grad_attn_weight: float32 [768, 4, 768], P(('crop', 'seq'))
- grad_out_weight: float32 [768, 768], P(('crop', 'seq'))
- grad_pair_gain: float32 [128], P(('crop', 'seq'))
- grad_pair_weight: float32 [128, 16], P(('crop', 'seq'))
- grad_expand_weight: float32 [768, 2, 1536], P(('crop', 'seq'))
- grad_contract_weight: float32 [1536, 768], P(('crop', 'seq'))
The draws below stay inside these ranges and needn't reach their ends.
Inputs may be any that keep to these rules, and one draw needn't show every extreme that they name: `segments`: within a crop the ids never fall; a crop holds 4 documents of 1 to 160 slots each. `pad_mask`: in each crop the real tokens form a prefix of at least 240 slots; the first crop has no padding.
All inputs are finite; a program needn't handle non-finite values.
Results may differ from the reference program's by a relative error of at most 0.012.
The reference program's roundings to bfloat16 on the way count: a program that leaves them out, or rounds other values in their place, can miss the bound.
Values may be sent and summed in bfloat16 or wider, within the bound.
A program may use at most 256 MiB of HBM per device.

```python
import math
import jax
import jax.numpy as jnp
import numpy as np
from jax import lax

C = 768
S = 384
PAIR_C = 128
H = 16
F = 1536
L = 320
DH = 48
CROPS = 16
TOKENS = 5120


def draw_pad_mask(key, part):
    lengths = jax.random.randint(key, (CROPS, 1), L - L // 4, L + 1)
    lengths = lengths.at[0, 0].set(L)
    places = jnp.arange(L, dtype=jnp.int32)[None, :]
    return (places < lengths).astype(jnp.int32)


def steps_of(stream_key, shape, shards, low, largest):
    factor_of, own = 1.0, jax.random.fold_in(stream_key, 6)
    for position, blocks in shards:
        draws = jnp.exp(jax.random.uniform(jax.random.fold_in(own, position), (blocks,), jnp.float32, low / len(shards), largest / len(shards)))
        factor_of = factor_of * jnp.repeat(draws, shape[position] // blocks).reshape([-1 if axis == position else 1 for axis in range(len(shape))])
    return factor_of


def length_profile(count, total, most, slope):
    loads = [(1 << 20) // math.isqrt(standing ** slope) + 1 for standing in range(2, count + 1)]
    spare, holding = total - most - (count - 1), [1] * (count - 1)
    while spare > 0:
        candidates = [i for i in range(count - 1) if holding[i] < most]
        mass, budget = sum([loads[i] for i in candidates]), spare
        for i in candidates:
            more = min(most - holding[i], max(1, budget * loads[i] // mass), spare)
            holding[i] = holding[i] + more
            spare = spare - more
    return np.array([most] + holding)


def ragged_sizes(key, count, total, most, slope):
    if count == 2:
        one = jax.random.randint(key, (), max(1, total - most), min(most, total - 1) + 1)
        return jnp.stack([one, total - one])
    sizes = jnp.asarray(length_profile(count, total, most, slope), jnp.int32)
    couples = (count - 1) // 2
    donor, receiver = sizes[1:1 + 2 * couples:2], sizes[2:2 + 2 * couples:2]
    room = jnp.minimum(donor - 1, most - receiver)
    shifted = jax.random.randint(jax.random.fold_in(key, 1), (couples,), 0, 1 << 20) % (room + 1)
    sizes = sizes.at[1:1 + 2 * couples:2].set(donor - shifted).at[2:2 + 2 * couples:2].set(receiver + shifted)
    return sizes[jax.random.permutation(jax.random.fold_in(key, 2), count)]


def normal_values(key, dims, width, bound, pieces=(), held_as=jnp.bfloat16):
    gain = steps_of(key, dims, pieces, -0.22, 0.18) if pieces else 1.0
    values = jax.random.normal(key, dims, jnp.float32) * width * gain
    return jnp.minimum(jnp.maximum(values, -bound), bound).astype(held_as)


def setup_inputs(seed: int = 0) -> dict:
    arg_keys = jax.random.split(jax.random.key(seed), 16)
    single = normal_values(arg_keys[0], (TOKENS, C), 1.0, 6.0, ((0, 32),))
    conditioning = normal_values(arg_keys[1], (TOKENS, S), 1.0, 6.0, ((0, 32),))
    pair_features = normal_values(arg_keys[2], (CROPS, L, L, PAIR_C), 1.0, 6.0, ((0, 16), (1, 2)))
    segments = jax.vmap(lambda own: jnp.searchsorted(jnp.cumsum(ragged_sizes(own, 4, L, L // 2, 1)), jnp.arange(L), side="right"))(jax.random.split(arg_keys[3], CROPS)).reshape((CROPS, L)).astype(jnp.int32)
    pad_mask = draw_pad_mask(jax.random.fold_in(arg_keys[15], 71), 0)
    cotangent = normal_values(arg_keys[5], (TOKENS, C), 1.0, 6.0, ((0, 32),))
    cond_gain = jnp.clip(1.0 + 0.18 * jax.random.normal(arg_keys[6], (S, 2), jnp.float32), 0.099609375, 1.8984375).astype(jnp.bfloat16)
    cond_weight = normal_values(arg_keys[7], (S, 6, C), S ** -0.5, 0.3125)
    biases = normal_values(arg_keys[8], (C, 5), 0.5, 3.0)
    attn_weight = normal_values(arg_keys[9], (C, 4, C), C ** -0.5, 0.21875)
    out_weight = normal_values(arg_keys[10], (C, C), (C // 64) ** -0.5, 1.75)
    pair_gain = jnp.clip(1.0 + 0.18 * jax.random.normal(arg_keys[11], (PAIR_C,), jnp.float32), 0.099609375, 1.8984375).astype(jnp.bfloat16)
    pair_weight = normal_values(arg_keys[12], (PAIR_C, H), PAIR_C ** -0.5, 0.5)
    expand_weight = normal_values(arg_keys[13], (C, 2, F), C ** -0.5, 0.21875)
    contract_weight = normal_values(arg_keys[14], (F, C), F ** -0.5, 0.15625)
    return {"single": single, "conditioning": conditioning, "pair_features": pair_features, "segments": segments, "pad_mask": pad_mask, "cotangent": cotangent, "cond_gain": cond_gain, "cond_weight": cond_weight, "biases": biases, "attn_weight": attn_weight, "out_weight": out_weight, "pair_gain": pair_gain, "pair_weight": pair_weight, "expand_weight": expand_weight, "contract_weight": contract_weight}


EPS = 1e-05
NEG = -1e+30
HIGH = lax.Precision.HIGHEST

@jax.custom_vjp
def low(v):
    return lax.optimization_barrier(v.astype(jnp.bfloat16)).astype(jnp.float32)

@jax.custom_vjp
def low_back(v):
    return v

def low_keep(v):
    return (low(v), None)

def low_pass(kept, grad):
    return (grad,)

def back_keep(v):
    return (v, None)

def back_low(kept, grad):
    return (low(grad),)
low.defvjp(low_keep, low_pass)
low_back.defvjp(back_keep, back_low)

def normed(values):
    centred = values - lax.optimization_barrier(jnp.mean(values, -1, keepdims=True))
    return centred * lax.rsqrt(lax.optimization_barrier(jnp.mean(centred * centred, -1, keepdims=True)) + EPS)

def matmul(left, right):
    return jnp.dot(left, right, precision=HIGH)

def crop_forward(segment_row, pad_row, single, conditioning, pair_features, cond_gain, cond_weight, biases, attn_weight, out_weight, pair_gain, pair_weight, expand_weight, contract_weight):
    crop_length = single.shape[0]
    single_norm = normed(single)
    cond_norm = normed(conditioning)
    modulated = []
    keep_gates = []
    for branch in range(2):
        cond_low = low(cond_norm * cond_gain[:, branch])
        scale_logit = low_back(matmul(cond_low, cond_weight[:, 3 * branch]) + biases[:, 2 * branch])
        shift_term = low_back(matmul(cond_low, cond_weight[:, 3 * branch + 1]))
        modulated.append(low(jax.nn.sigmoid(scale_logit) * single_norm + shift_term))
        keep_logit = low_back(matmul(conditioning, cond_weight[:, 3 * branch + 2]) + biases[:, 2 * branch + 1])
        keep_gates.append(jax.nn.sigmoid(keep_logit))
    attn_in = modulated[0]
    trans_in = modulated[1]
    queries = low_back(low(matmul(attn_in, attn_weight[:, 0]) + biases[:, 4])).reshape(crop_length, H, DH)
    keys_all = low_back(low(matmul(attn_in, attn_weight[:, 1]))).reshape(crop_length, H, DH)
    values_all = low_back(low(matmul(attn_in, attn_weight[:, 2]))).reshape(crop_length, H, DH)
    attn_gate = jax.nn.sigmoid(low_back(matmul(attn_in, attn_weight[:, 3])))
    pair_low = low(normed(pair_features) * pair_gain)
    pair_bias = low_back(low(jnp.einsum('ijc,ch->ihj', pair_low, pair_weight, precision=HIGH)))
    raw_scores = jnp.einsum('qhd,khd->qhk', queries, keys_all, precision=HIGH) * (1.0 / math.sqrt(DH))
    scores = low_back(raw_scores + pair_bias)
    places = jnp.arange(crop_length, dtype=jnp.int32)
    allowed = (segment_row[:, None] == segment_row[None, :]) & ((pad_row[None, :] == 1) | (places[:, None] == places[None, :]))
    softmax_weights = jax.nn.softmax(jnp.where(allowed[:, None, :], scores, NEG), axis=-1)
    attended = low_back(low(jnp.einsum('qhk,khd->qhd', low(softmax_weights), values_all, precision=HIGH)))
    gated_mix = low(attended.reshape(crop_length, C) * attn_gate)
    attn_out = low_back(matmul(gated_mix, out_weight))
    hidden_pre = jnp.einsum('tc,cke->tke', trans_in, expand_weight, precision=HIGH)
    gate_pre = low_back(hidden_pre[:, 0])
    up_pre = low_back(hidden_pre[:, 1])
    hidden = low(jax.nn.silu(gate_pre) * up_pre)
    trans_out = low_back(matmul(hidden, contract_weight))
    return single + keep_gates[0] * attn_out + keep_gates[1] * trans_out

def reference(single, conditioning, pair_features, segments, pad_mask, cotangent, cond_gain, cond_weight, biases, attn_weight, out_weight, pair_gain, pair_weight, expand_weight, contract_weight):
    weights = tuple((member.astype(jnp.float32) for member in (cond_gain, cond_weight, biases, attn_weight, out_weight, pair_gain, pair_weight, expand_weight, contract_weight)))
    by_crop = (single.reshape(CROPS, L, C), conditioning.reshape(CROPS, L, S), pair_features, segments, pad_mask, cotangent.reshape(CROPS, L, C))

    def one_crop(totals, crop_data):
        single_crop, cond_crop, pair_crop, segment_row, pad_row, upstream = crop_data

        def forward(*operands):
            return crop_forward(segment_row, pad_row, *operands)
        result, pullback = jax.vjp(forward, single_crop.astype(jnp.float32), cond_crop.astype(jnp.float32), pair_crop.astype(jnp.float32), *weights)
        gradients = pullback(upstream.astype(jnp.float32))
        totals = tuple((running + gradient for running, gradient in zip(totals, gradients[3:])))
        return (totals, (result.astype(jnp.bfloat16), gradients[0], gradients[1], gradients[2].astype(jnp.bfloat16)))
    initial = tuple((jnp.zeros_like(member) for member in weights))
    totals, outputs = lax.scan(one_crop, initial, by_crop)
    result, grad_single, grad_cond, grad_pair = outputs
    return (result.reshape(TOKENS, C), grad_single.reshape(TOKENS, C), grad_cond.reshape(TOKENS, S), grad_pair, totals[0], totals[1], totals[2], totals[3], totals[4], totals[5], totals[6], totals[7], totals[8])
```

```python
import functools
import math
import jax
import jax.numpy as jnp
from jax import lax
from jax.experimental import pallas as pl
from jax.experimental.pallas import tpu as pltpu
from jax.sharding import PartitionSpec as P

EPS = 1e-05
NEG = -1e30
F32 = jnp.float32
BF16 = jnp.bfloat16


def dot_nt(a, b):
    return lax.dot_general(a, b, (((1,), (1,)), ((), ())), preferred_element_type=F32)


def dot_tn(a, b):
    return lax.dot_general(a, b, (((0,), (0,)), ((), ())), preferred_element_type=F32)


def dot_nn(a, b):
    return jnp.dot(a, b, preferred_element_type=F32)


def split3(v):
    hi = v.astype(BF16)
    rest = v - hi.astype(F32)
    mid = rest.astype(BF16)
    lo = (rest - mid.astype(F32)).astype(BF16)
    return hi, mid, lo


def pair_fwd_kernel(x_ref, w_ref, bias_ref, inv_ref, mean_ref):
    rows, keys, chan = x_ref.shape
    heads = bias_ref.shape[0]
    w = w_ref[...]
    ones = jnp.full((8, chan), 1.0, BF16)
    spread = jnp.full((chan, chan), 1.0 / chan, BF16)
    for base in range(0, rows, 8):
        parts = []
        invs = []
        means = []
        for i in range(base, base + 8):
            x = x_ref[i]
            raw = dot_nt(w, x)
            mean = raw[3 * heads : 3 * heads + 1] * (1.0 / chan)
            centred = x.astype(F32) - dot_nn(x, spread)
            square = (centred * centred).astype(BF16)
            var = dot_nt(ones, square)[0:1] * (1.0 / chan)
            inv = lax.rsqrt(var + EPS)
            parts.append((raw[:heads] + raw[heads : 2 * heads] + raw[2 * heads : 3 * heads]) * inv)
            invs.append(inv)
            means.append(mean)
        block = jnp.stack(parts, axis=0)
        bias_ref[:, base : base + 8, :] = pltpu.einshape("ihj->hij", block).astype(BF16)
        inv_ref[base : base + 8, :] = jnp.concatenate(invs, axis=0)
        mean_ref[base : base + 8, :] = jnp.concatenate(means, axis=0)


def pair_fwd(x, w, heads, tile=16):
    rows, keys, chan = x.shape
    return pl.pallas_call(
        pair_fwd_kernel,
        grid=(rows // tile,),
        in_specs=[
            pl.BlockSpec((tile, keys, chan), lambda i: (i, 0, 0)),
            pl.BlockSpec(w.shape, lambda i: (0, 0)),
        ],
        out_specs=[
            pl.BlockSpec((heads, tile, keys), lambda i: (0, i, 0)),
            pl.BlockSpec((tile, keys), lambda i: (i, 0)),
            pl.BlockSpec((tile, keys), lambda i: (i, 0)),
        ],
        out_shape=[
            jax.ShapeDtypeStruct((heads, rows, keys), BF16),
            jax.ShapeDtypeStruct((rows, keys), F32),
            jax.ShapeDtypeStruct((rows, keys), F32),
        ],
        cost_estimate=pl.CostEstimate(flops=0, transcendentals=0, bytes_accessed=96 << 20),
        name="pair_fwd",
    )(x, w)


def attn_kernel(half_ref, q_ref, kvo_ref, kvr_ref, ga_ref, bias_ref, inv_ref, mean_ref,
                segc_ref, segr_ref, padr_ref,
                att_ref, dq_ref, own_ref, send_ref, r_ref, t_ref, s_ref, k_sc, v_sc, m2_sc, dk_sc, dv_sc):
    rows = q_ref.shape[0]
    heads, _, keys = bias_ref.shape
    size = q_ref.shape[1] // heads
    scale = 1.0 / math.sqrt(size)
    half = half_ref[0]
    own = pl.ds(pl.multiple_of(half * rows, 32), rows)
    other = pl.ds(pl.multiple_of((1 - half) * rows, 32), rows)
    width = q_ref.shape[1]
    k_sc[own, :] = kvo_ref[:, :width]
    k_sc[other, :] = kvr_ref[:, :width]
    v_sc[own, :] = kvo_ref[:, width:]
    v_sc[other, :] = kvr_ref[:, width:]
    row_id = lax.broadcasted_iota(jnp.int32, (rows, keys), 0) + half * rows
    col_id = lax.broadcasted_iota(jnp.int32, (rows, keys), 1)
    allowed = (segc_ref[...] == segr_ref[...]) & ((padr_ref[...] == 1) | (row_id == col_id))
    m2_sc[...] = jnp.where(allowed, 0.0, NEG)
    inv = inv_ref[...]
    m2 = jnp.zeros((rows, keys), F32)
    for h in range(heads):
        cut = slice(h * size, (h + 1) * size)
        qh = q_ref[:, cut]
        kh = k_sc[:, cut]
        vh = v_sc[:, cut]
        gh = ga_ref[:, cut]
        bias = bias_ref[h].astype(F32)
        scores = dot_nt(qh, kh) * scale + bias + m2_sc[...]
        top = jnp.max(scores, axis=-1, keepdims=True)
        e = jnp.exp(scores - top)
        p = e * (1.0 / jnp.sum(e, axis=-1, keepdims=True))
        low = p.astype(BF16)
        att_ref[:, cut] = dot_nn(low, vh).astype(BF16)
        gp = dot_nt(gh, vh)
        pg = p * gp
        delta = jnp.sum(pg, axis=-1, keepdims=True)
        gs32 = pg - p * delta
        gs = gs32.astype(BF16)
        dq_ref[:, cut] = (dot_nn(gs, kh) * scale).astype(BF16)
        dk_sc[:, cut] = dot_tn(gs, qh) * scale
        dv_sc[:, cut] = dot_tn(low, gh)
        m2 = m2 + gs32 * bias
        r_ref[h] = (gs.astype(F32) * inv).astype(BF16)
    own_ref[:, :width] = dk_sc[own, :]
    own_ref[:, width:] = dv_sc[own, :]
    send_ref[:, :width] = dk_sc[other, :]
    send_ref[:, width:] = dv_sc[other, :]
    chan = 128.0
    slope = inv * inv * m2 * (1.0 / chan)
    s_ref[...] = -slope
    t_ref[...] = slope * mean_ref[...]


def attention(half, q, kvo, kvr, ga, bias, inv, mean, segc, segr, padr):
    rows, width = q.shape
    heads, _, keys = bias.shape
    vm = pl.BlockSpec(memory_space=pltpu.VMEM)
    return pl.pallas_call(
        attn_kernel,
        in_specs=[pl.BlockSpec(memory_space=pltpu.SMEM)] + [vm] * 10,
        out_specs=[vm] * 7,
        out_shape=[
            jax.ShapeDtypeStruct((rows, width), BF16),
            jax.ShapeDtypeStruct((rows, width), BF16),
            jax.ShapeDtypeStruct((rows, 2 * width), F32),
            jax.ShapeDtypeStruct((rows, 2 * width), F32),
            jax.ShapeDtypeStruct((heads, rows, keys), BF16),
            jax.ShapeDtypeStruct((rows, keys), F32),
            jax.ShapeDtypeStruct((rows, keys), F32),
        ],
        scratch_shapes=[
            pltpu.VMEM((keys, width), BF16),
            pltpu.VMEM((keys, width), BF16),
            pltpu.VMEM((rows, keys), F32),
            pltpu.VMEM((keys, width), F32),
            pltpu.VMEM((keys, width), F32),
        ],
        cost_estimate=pl.CostEstimate(flops=0, transcendentals=0, bytes_accessed=64 << 20),
        name="attn",
    )(half, q, kvo, kvr, ga, bias, inv, mean, segc, segr, padr)


def pair_bwd_kernel(x_ref, r_ref, t_ref, s_ref, mean_ref, w_ref, out_ref, n_ref, c_ref):
    rows, keys, chan = x_ref.shape
    heads = r_ref.shape[0]
    depth = w_ref.shape[0]
    w = w_ref[...]

    @pl.when(pl.program_id(0) == 0)
    def _():
        n_ref[...] = jnp.zeros_like(n_ref)
        c_ref[...] = jnp.zeros_like(c_ref)

    acc = jnp.zeros(n_ref.shape, F32)
    corr = jnp.zeros(c_ref.shape, F32)
    pad = jnp.zeros((depth - 2 * heads - 6, keys), F32)
    for base in range(0, rows, 8):
        block = pltpu.einshape("hij->ihj", r_ref[:, base : base + 8, :].astype(F32))
        for k in range(8):
            i = base + k
            r32 = block[k]
            t = t_ref[i : i + 1, :]
            s = s_ref[i : i + 1, :]
            th, tm, tl = (v.astype(F32) for v in split3(t))
            sh, sm, sl = (v.astype(F32) for v in split3(s))
            left = jnp.concatenate([r32, r32, th, tm, tl, sh, sm, sl, pad], axis=0).astype(BF16)
            both = dot_tn(left, w)
            x = x_ref[i]
            out_ref[i] = (both[:, :chan] + x.astype(F32) * both[:, chan:]).astype(BF16)
            acc = acc + dot_nn(r32.astype(BF16), x)
            corr = corr + r32 * mean_ref[i : i + 1, :]
    n_ref[...] += acc
    c_ref[...] += corr


def pair_bwd(x, r, t, s, mean, w, tile=16):
    rows, keys, chan = x.shape
    heads = r.shape[0]
    return pl.pallas_call(
        pair_bwd_kernel,
        grid=(rows // tile,),
        in_specs=[
            pl.BlockSpec((tile, keys, chan), lambda i: (i, 0, 0)),
            pl.BlockSpec((heads, tile, keys), lambda i: (0, i, 0)),
            pl.BlockSpec((tile, keys), lambda i: (i, 0)),
            pl.BlockSpec((tile, keys), lambda i: (i, 0)),
            pl.BlockSpec((tile, keys), lambda i: (i, 0)),
            pl.BlockSpec(w.shape, lambda i: (0, 0)),
        ],
        out_specs=[
            pl.BlockSpec((tile, keys, chan), lambda i: (i, 0, 0)),
            pl.BlockSpec((heads, chan), lambda i: (0, 0)),
            pl.BlockSpec((heads, keys), lambda i: (0, 0)),
        ],
        out_shape=[
            jax.ShapeDtypeStruct((rows, keys, chan), BF16),
            jax.ShapeDtypeStruct((heads, chan), F32),
            jax.ShapeDtypeStruct((heads, keys), F32),
        ],
        cost_estimate=pl.CostEstimate(flops=0, transcendentals=0, bytes_accessed=60 << 20),
        name="pair_bwd",
    )(x, r, t, s, mean, w)


def norm_rows(values):
    centred = values - jnp.mean(values, -1, keepdims=True)
    inverse = lax.rsqrt(jnp.mean(centred * centred, -1, keepdims=True) + EPS)
    return (centred * inverse, inverse)


def norm_back(incoming, normal, inverse):
    return inverse * (
        incoming
        - jnp.mean(incoming, -1, keepdims=True)
        - normal * jnp.mean(incoming * normal, -1, keepdims=True)
    )


def sigmoid(v):
    return jax.nn.sigmoid(v)


def fetch(pairs, sems):
    copies = [pltpu.make_async_copy(src, dst, sems.at[k]) for k, (src, dst) in enumerate(pairs)]
    for copy in copies:
        copy.start()
    return copies


def front_kernel(
    single_ref, cond_ref, gain_ref, bias_ref, pair_gain_ref, pair_weight_ref, cw_hbm, aw_hbm,
    x_ref, q_ref, kv_ref, scale0_ref, scale1_ref, keep0_ref, keep1_ref, forward_ref, backward_ref,
    cw, aw, sems,
):
    copies = fetch(
        [(cw_hbm.at[k], cw.at[k]) for k in range(6)] + [(aw_hbm.at[k], aw.at[k]) for k in range(3)], sems
    )
    width = single_ref.shape[1]
    cond_width = cond_ref.shape[1]
    gained = pair_weight_ref[...].astype(F32) * pair_gain_ref[...].astype(F32)
    heads, chan = gained.shape
    hi, mid, lo = split3(gained - jnp.mean(gained, axis=1, keepdims=True))
    forward_ref[0:heads, :] = hi
    forward_ref[heads : 2 * heads, :] = mid
    forward_ref[2 * heads : 3 * heads, :] = lo
    row = lax.broadcasted_iota(jnp.int32, (16, chan), 0)
    forward_ref[3 * heads :, :] = jnp.where(row == 0, 1.0, 0.0).astype(BF16)
    backward_ref[0:heads, :chan] = hi
    backward_ref[heads : 2 * heads, :chan] = mid
    backward_ref[0 : 2 * heads, chan:] = jnp.zeros((2 * heads, chan), BF16)
    backward_ref[2 * heads :, :chan] = jnp.where(row < 3, 1.0, 0.0).astype(BF16)
    backward_ref[2 * heads :, chan:] = jnp.where((row >= 3) & (row < 6), 1.0, 0.0).astype(BF16)

    single_norm, _ = norm_rows(single_ref[...].astype(F32))
    cond_norm, _ = norm_rows(cond_ref[...].astype(F32))
    cond = cond_ref[...]
    x_ref[:, 2 * width + 2 * cond_width :] = cond
    for b, scale_ref, keep_ref in ((0, scale0_ref, keep0_ref), (1, scale1_ref, keep1_ref)):
        low = (cond_norm * gain_ref[b : b + 1, :].astype(F32)).astype(BF16)
        x_ref[:, 2 * width + b * cond_width : 2 * width + (b + 1) * cond_width] = low
        copies[3 * b].wait()
        scale = sigmoid(dot_nn(low, cw[3 * b]) + bias_ref[2 * b : 2 * b + 1, :].astype(F32))
        scale_ref[...] = scale
        copies[3 * b + 1].wait()
        shift = dot_nn(low, cw[3 * b + 1])
        x_ref[:, b * width : (b + 1) * width] = (scale * single_norm + shift).astype(BF16)
        copies[3 * b + 2].wait()
        keep_ref[...] = sigmoid(
            dot_nn(cond, cw[3 * b + 2]) + bias_ref[2 * b + 1 : 2 * b + 2, :].astype(F32)
        )
    attn_in = x_ref[:, :width]
    copies[6].wait()
    q_ref[...] = (dot_nn(attn_in, aw[0]) + bias_ref[4:5, :].astype(F32)).astype(BF16)
    copies[7].wait()
    kv_ref[:, :width] = dot_nn(attn_in, aw[1]).astype(BF16)
    copies[8].wait()
    kv_ref[:, width:] = dot_nn(attn_in, aw[2]).astype(BF16)


def front(single, cond, gains, biases, pair_gain, pair_weight, cw, aw):
    rows, width = single.shape
    cond_width = cond.shape[1]
    heads, chan = pair_weight.shape
    vm = pl.BlockSpec(memory_space=pltpu.VMEM)
    hbm = pl.BlockSpec(memory_space=pl.ANY)
    wide = jax.ShapeDtypeStruct((rows, width), F32)
    return pl.pallas_call(
        front_kernel,
        in_specs=[vm] * 6 + [hbm] * 2,
        out_specs=[vm] * 9,
        out_shape=[
            jax.ShapeDtypeStruct((rows, 2 * width + 3 * cond_width), BF16),
            jax.ShapeDtypeStruct((rows, width), BF16),
            jax.ShapeDtypeStruct((rows, 2 * width), BF16),
            wide, wide, wide, wide,
            jax.ShapeDtypeStruct((3 * heads + 16, chan), BF16),
            jax.ShapeDtypeStruct((2 * heads + 16, 2 * chan), BF16),
        ],
        scratch_shapes=[
            pltpu.VMEM(cw.shape, BF16),
            pltpu.VMEM((3,) + aw.shape[1:], BF16),
            pltpu.SemaphoreType.DMA((9,)),
        ],
        cost_estimate=pl.CostEstimate(flops=0, transcendentals=0, bytes_accessed=36 << 20),
        name="front",
    )(single, cond, gains, biases, pair_gain, pair_weight, cw, aw)


def put(side, own_ref, send_ref, start, low, high):
    stop = start + low.shape[1]

    @pl.when(side == 0)
    def _():
        own_ref[:, start:stop] = low
        send_ref[:, start:stop] = high

    @pl.when(side != 0)
    def _():
        own_ref[:, start:stop] = high
        send_ref[:, start:stop] = low


def total(v):
    return jnp.sum(v.astype(F32), axis=0, keepdims=True)


def trans_kernel(
    side_ref, x_ref, single_ref, cond_ref, cot_ref, gain_ref, scale_ref, keep_ref, ew_hbm, tw_hbm, cw_hbm,
    own_ref, send_ref, kept_ref, grad_norm_ref, grad_cond_ref, grad_direct_ref, sums_ref, gain_sum_ref,
    ew, tw, cw, sems,
):
    copies = fetch(
        [(ew_hbm.at[0], ew.at[0]), (ew_hbm.at[1], ew.at[1]), (tw_hbm, tw)]
        + [(cw_hbm.at[3 + k], cw.at[k]) for k in range(3)],
        sems,
    )
    side = side_ref[0]
    rows, width = single_ref.shape
    cut = width // 2
    hidden_width = tw.shape[0]
    trans_in = x_ref[:, width : 2 * width]
    upstream = cot_ref[...].astype(F32)
    keep = keep_ref[...]
    grad_trans = (upstream * keep).astype(BF16)
    at = hidden_width
    put(side, own_ref, send_ref, at + hidden_width, grad_trans[:, :cut], grad_trans[:, cut:])
    copies[0].wait()
    copies[1].wait()
    copies[2].wait()
    grad_in = jnp.zeros((rows, width), F32)
    trans_out = jnp.zeros((rows, width), F32)
    step = 512
    for c in range(0, hidden_width, step):
        span = slice(c, c + step)
        gate_pre = dot_nn(trans_in, ew[0, :, span])
        up_pre = dot_nn(trans_in, ew[1, :, span])
        sig = sigmoid(gate_pre)
        act = gate_pre * sig
        hidden = (act * up_pre).astype(BF16)
        own_ref[:, span] = hidden
        send_ref[:, span] = hidden
        trans_out = trans_out + dot_nn(hidden, tw[span, :])
        grad_hidden = dot_nt(grad_trans, tw[span, :])
        grad_gate = (grad_hidden * up_pre * sig * (1.0 + gate_pre * (1.0 - sig))).astype(BF16)
        grad_up = (grad_hidden * act).astype(BF16)
        put(side, own_ref, send_ref, at + c, grad_gate, grad_up)
        grad_in = grad_in + dot_nt(grad_gate, ew[0, :, span]) + dot_nt(grad_up, ew[1, :, span])
    kept_ref[...] = keep * trans_out
    grad_keep = (upstream * trans_out * keep * (1.0 - keep)).astype(BF16)
    at = 2 * hidden_width + cut
    finish_branch(
        side, 1, at, copies[3:], cw, single_ref, cond_ref, gain_ref, scale_ref, grad_in, grad_keep,
        own_ref, send_ref, grad_norm_ref, grad_cond_ref, grad_direct_ref, sums_ref, gain_sum_ref,
    )


def finish_branch(
    side, b, at, copies, cw, single_ref, cond_ref, gain_ref, scale_ref, grad_in, grad_keep,
    own_ref, send_ref, grad_norm_ref, grad_cond_ref, grad_direct_ref, sums_ref, gain_sum_ref,
):
    width = single_ref.shape[1]
    cut = width // 2
    single_norm, _ = norm_rows(single_ref[...].astype(F32))
    cond_norm, _ = norm_rows(cond_ref[...].astype(F32))
    scale = scale_ref[...]
    grad_scale = (grad_in * single_norm * scale * (1.0 - scale)).astype(BF16)
    grad_shift = grad_in.astype(BF16)
    put(side, own_ref, send_ref, at, grad_scale, grad_shift)
    put(side, own_ref, send_ref, at + width, grad_keep[:, :cut], grad_keep[:, cut:])
    grad_norm_ref[...] = grad_in * scale
    for copy in copies:
        copy.wait()
    grad_low = dot_nt(grad_scale, cw[0]) + dot_nt(grad_shift, cw[1])
    grad_cond_ref[...] = grad_low * gain_ref[b : b + 1, :].astype(F32)
    grad_direct_ref[...] = dot_nt(grad_keep, cw[2])
    gain_sum_ref[...] = total(grad_low * cond_norm)
    sums_ref[0:1, :] = total(grad_scale)
    sums_ref[1:2, :] = total(grad_keep)


def branch_outputs(rows, width, cond_width, packed):
    return [
        jax.ShapeDtypeStruct((rows, packed), BF16),
        jax.ShapeDtypeStruct((rows, packed), BF16),
    ]


def trans(side, x, single, cond, cot, gains, scale, keep, ew, tw, cw):
    rows, width = single.shape
    cond_width = cond.shape[1]
    hidden_width = tw.shape[0]
    packed = 2 * hidden_width + width // 2 + width + width // 2
    vm = pl.BlockSpec(memory_space=pltpu.VMEM)
    hbm = pl.BlockSpec(memory_space=pl.ANY)
    return pl.pallas_call(
        trans_kernel,
        in_specs=[pl.BlockSpec(memory_space=pltpu.SMEM)] + [vm] * 7 + [hbm] * 3,
        out_specs=[vm] * 8,
        out_shape=[
            jax.ShapeDtypeStruct((rows, packed), BF16),
            jax.ShapeDtypeStruct((rows, packed), BF16),
            jax.ShapeDtypeStruct((rows, width), F32),
            jax.ShapeDtypeStruct((rows, width), F32),
            jax.ShapeDtypeStruct((rows, cond_width), F32),
            jax.ShapeDtypeStruct((rows, cond_width), F32),
            jax.ShapeDtypeStruct((2, width), F32),
            jax.ShapeDtypeStruct((1, cond_width), F32),
        ],
        scratch_shapes=[
            pltpu.VMEM(ew.shape, BF16),
            pltpu.VMEM(tw.shape, BF16),
            pltpu.VMEM((3,) + cw.shape[1:], BF16),
            pltpu.SemaphoreType.DMA((6,)),
        ],
        cost_estimate=pl.CostEstimate(flops=0, transcendentals=0, bytes_accessed=50 << 20),
        name="trans",
    )(side, x, single, cond, cot, gains, scale, keep, ew, tw, cw)


def middle_kernel(x_ref, cot_ref, keep_ref, aw_hbm, ow_hbm, gate_ref, mixed_ref, attended_ref, aw, ow, sems):
    copies = fetch([(aw_hbm.at[3], aw), (ow_hbm, ow)], sems)
    width = cot_ref.shape[1]
    copies[0].wait()
    gate = sigmoid(dot_nn(x_ref[:, :width], aw[...]))
    gate_ref[...] = gate
    grad_attn = (cot_ref[...].astype(F32) * keep_ref[...]).astype(BF16)
    copies[1].wait()
    grad_mixed = dot_nt(grad_attn, ow[...])
    mixed_ref[...] = grad_mixed
    attended_ref[...] = (grad_mixed * gate).astype(BF16)


def middle(x, cot, keep, aw, ow):
    rows, width = cot.shape
    vm = pl.BlockSpec(memory_space=pltpu.VMEM)
    hbm = pl.BlockSpec(memory_space=pl.ANY)
    return pl.pallas_call(
        middle_kernel,
        in_specs=[vm] * 3 + [hbm] * 2,
        out_specs=[vm] * 3,
        out_shape=[
            jax.ShapeDtypeStruct((rows, width), F32),
            jax.ShapeDtypeStruct((rows, width), F32),
            jax.ShapeDtypeStruct((rows, width), BF16),
        ],
        scratch_shapes=[
            pltpu.VMEM(aw.shape[1:], BF16),
            pltpu.VMEM(ow.shape, BF16),
            pltpu.SemaphoreType.DMA((2,)),
        ],
        cost_estimate=pl.CostEstimate(flops=0, transcendentals=0, bytes_accessed=12 << 20),
        name="middle",
    )(x, cot, keep, aw, ow)


def after_kernel(
    side_ref, x_ref, single_ref, cond_ref, cot_ref, gain_ref, scale_ref, keep_ref, gate_ref, grad_mixed_ref,
    attended_ref, grad_q_ref, dkv_own_ref, dkv_recv_ref, kept_ref, grad_norm1_ref, grad_cond1_ref, direct1_ref,
    aw_hbm, ow_hbm, cw_hbm,
    own_ref, send_ref, layer_ref, grad_single_ref, grad_cond_ref, sums_ref, gain_sum_ref,
    aw, ow, cw, norm_sc, cond_sc, direct_sc, sems,
):
    copies = fetch(
        [(ow_hbm, ow)] + [(aw_hbm.at[k], aw.at[k]) for k in range(4)] + [(cw_hbm.at[k], cw.at[k]) for k in range(3)],
        sems,
    )
    side = side_ref[0]
    width = single_ref.shape[1]
    cut = width // 2
    upstream = cot_ref[...].astype(F32)
    keep = keep_ref[...]
    gate = gate_ref[...]
    attended = attended_ref[...].astype(F32)
    mixed = (attended * gate).astype(BF16)
    own_ref[:, :width] = mixed
    send_ref[:, :width] = mixed
    grad_q = grad_q_ref[...]
    grad_k = (dkv_own_ref[:, :width] + dkv_recv_ref[:, :width]).astype(BF16)
    grad_v = (dkv_own_ref[:, width:] + dkv_recv_ref[:, width:]).astype(BF16)
    grad_logit = (grad_mixed_ref[...] * attended * gate * (1.0 - gate)).astype(BF16)
    put(side, own_ref, send_ref, width, grad_q, grad_v)
    put(side, own_ref, send_ref, 2 * width, grad_k, grad_logit)
    grad_attn = (upstream * keep).astype(BF16)
    put(side, own_ref, send_ref, 3 * width, grad_attn[:, :cut], grad_attn[:, cut:])
    copies[0].wait()
    attn_out = dot_nn(mixed, ow[...])
    layer_ref[...] = (single_ref[...].astype(F32) + keep * attn_out + kept_ref[...]).astype(BF16)
    grad_keep = (upstream * attn_out * keep * (1.0 - keep)).astype(BF16)
    grad_in = jnp.zeros(single_ref.shape, F32)
    for k, part in enumerate((grad_q, grad_k, grad_v, grad_logit)):
        copies[1 + k].wait()
        grad_in = grad_in + dot_nt(part, aw[k])
    finish_branch(
        side, 0, 3 * width + cut, copies[5:], cw, single_ref, cond_ref, gain_ref, scale_ref, grad_in, grad_keep,
        own_ref, send_ref, norm_sc, cond_sc, direct_sc, sums_ref, gain_sum_ref,
    )
    sums_ref[2:3, :] = total(grad_q)
    single_norm, single_inverse = norm_rows(single_ref[...].astype(F32))
    cond_norm, cond_inverse = norm_rows(cond_ref[...].astype(F32))
    grad_single_ref[...] = upstream + norm_back(norm_sc[...] + grad_norm1_ref[...], single_norm, single_inverse)
    grad_cond_ref[...] = (
        norm_back(cond_sc[...] + grad_cond1_ref[...], cond_norm, cond_inverse) + (direct_sc[...] + direct1_ref[...])
    )


def after(side, x, single, cond, cot, gains, scale, keep, gate, grad_mixed, attended, grad_q, dkv_own, dkv_recv,
          kept, grad_norm1, grad_cond1, direct1, aw, ow, cw):
    rows, width = single.shape
    cond_width = cond.shape[1]
    packed = 3 * width + width // 2 + width + width // 2
    vm = pl.BlockSpec(memory_space=pltpu.VMEM)
    hbm = pl.BlockSpec(memory_space=pl.ANY)
    return pl.pallas_call(
        after_kernel,
        in_specs=[pl.BlockSpec(memory_space=pltpu.SMEM)] + [vm] * 17 + [hbm] * 3,
        out_specs=[vm] * 7,
        out_shape=[
            jax.ShapeDtypeStruct((rows, packed), BF16),
            jax.ShapeDtypeStruct((rows, packed), BF16),
            jax.ShapeDtypeStruct((rows, width), BF16),
            jax.ShapeDtypeStruct((rows, width), F32),
            jax.ShapeDtypeStruct((rows, cond_width), F32),
            jax.ShapeDtypeStruct((3, width), F32),
            jax.ShapeDtypeStruct((1, cond_width), F32),
        ],
        scratch_shapes=[
            pltpu.VMEM(aw.shape, BF16),
            pltpu.VMEM(ow.shape, BF16),
            pltpu.VMEM((3,) + cw.shape[1:], BF16),
            pltpu.VMEM((rows, width), F32),
            pltpu.VMEM((rows, cond_width), F32),
            pltpu.VMEM((rows, cond_width), F32),
            pltpu.SemaphoreType.DMA((8,)),
        ],
        cost_estimate=pl.CostEstimate(flops=0, transcendentals=0, bytes_accessed=40 << 20),
        name="after",
    )(side, x, single, cond, cot, gains, scale, keep, gate, grad_mixed, attended, grad_q, dkv_own, dkv_recv,
      kept, grad_norm1, grad_cond1, direct1, aw, ow, cw)


TILE = 384


def place(position, order):
    count = len(order)
    return sum(((position >> (count - 1 - j)) & 1) << order[j] for j in range(count))


def wgrad_kernel(plan, orders, me_ref, x_own, x_recv, g_own, g_recv, *refs):
    outs, (turned_ref,) = refs[:4], refs[4:]
    me = me_ref[0]
    blocks = 1 << len(orders[0])
    for source, start, width, uses in plan:
        height = width // blocks
        own, recv = ((x_own, x_recv), (g_own, g_recv))[source]
        span = slice(start, start + width)
        turned_ref[:width, :] = jnp.concatenate([own[:, span], recv[:, span]], axis=0).astype(F32).T
        for color in (0, 1):
            mine = [use for use in uses if use[1] == color]
            if not mine:
                continue
            left = jnp.concatenate(
                [
                    turned_ref[pl.ds(pl.multiple_of((me ^ place(p, orders[color])) * height, 8), height), :]
                    for p in range(blocks)
                ],
                axis=0,
            ).astype(BF16)
            keep_ref, send_ref = outs[2 * color], outs[2 * color + 1]
            for column, _, offset in mine:
                cut = slice(column, column + TILE)
                term = dot_nn(left, jnp.concatenate([g_own[:, cut], g_recv[:, cut]], axis=0))
                for p in range(blocks):
                    piece = term[p * height : (p + 1) * height]
                    if p < blocks // 2:
                        keep_ref[p, offset : offset + height, :] = piece
                    else:
                        send_ref[p - blocks // 2, offset : offset + height, :] = piece.astype(BF16)


def wgrad(me, x_own, x_recv, g_own, g_recv, plan, orders, totals, name):
    rows = x_own.shape[0]
    blocks = 1 << len(orders[0])
    half = blocks // 2
    if any((width // blocks) % 8 for _, _, width, _ in plan):
        return wgrad_plain(me, x_own, x_recv, g_own, g_recv, plan, orders)
    vm = pl.BlockSpec(memory_space=pltpu.VMEM)
    out_shape = []
    for count in totals:
        out_shape.append(jax.ShapeDtypeStruct((half, count, TILE), F32))
        out_shape.append(jax.ShapeDtypeStruct((half, count, TILE), BF16))
    widest = max(group[2] for group in plan)
    return pl.pallas_call(
        functools.partial(wgrad_kernel, plan, orders),
        in_specs=[pl.BlockSpec(memory_space=pltpu.SMEM)] + [vm] * 4,
        out_specs=[vm] * 4,
        out_shape=out_shape,
        scratch_shapes=[pltpu.VMEM((widest, 2 * rows), F32)],
        cost_estimate=pl.CostEstimate(flops=0, transcendentals=0, bytes_accessed=28 << 20),
        name=name,
    )(me, x_own, x_recv, g_own, g_recv)


def wgrad_plain(me, x_own, x_recv, g_own, g_recv, plan, orders):
    blocks = 1 << len(orders[0])
    pieces = ([], [])
    for source, start, width, uses in plan:
        own, recv = ((x_own, x_recv), (g_own, g_recv))[source]
        x = jnp.concatenate([own[:, start : start + width], recv[:, start : start + width]], axis=0)
        for column, color, _ in uses:
            g = jnp.concatenate([g_own[:, column : column + TILE], g_recv[:, column : column + TILE]], axis=0)
            wanted = jnp.stack([me[0] ^ place(p, orders[color]) for p in range(blocks)])
            pieces[color].append(jnp.take(dot_tn(x, g).reshape(blocks, width // blocks, TILE), wanted, axis=0))
    outs = []
    for parts in pieces:
        whole = jnp.concatenate(parts, axis=1)
        outs += [whole[: blocks // 2], whole[blocks // 2 :].astype(BF16)]
    return outs


def layout(groups, blocks, column):
    offsets = [0, 0]
    plan = []
    for source, start, width, colors in groups:
        uses = []
        for color in colors:
            uses.append((column, color, offsets[color]))
            column += TILE
            offsets[color] += width // blocks
        plan.append((source, start, width, tuple(uses)))
    return tuple(plan), tuple(offsets)


def send_half(value, bit):
    count = lax.axis_size("crop")
    return lax.ppermute(value, "crop", [(i, i ^ (1 << bit)) for i in range(count)])


def arrivals(state, j, orders):
    return [send_half(send, order[j]) for (_, send), order in zip(state, orders)]


def added(state, arrived):
    out = []
    for (keep, send), other in zip(state, arrived):
        whole = keep.astype(F32) + other.astype(F32)
        half = whole.shape[0] // 2
        out.append((whole[:half], whole[half:].astype(send.dtype)) if half else (whole[0], None))
    return out


def swap(v):
    return lax.ppermute(v, "seq", [(0, 1), (1, 0)])


def rows_of(side, ref, offset, height):
    v = ref[offset : offset + height, :]
    return jnp.where(side == 0, v[: height // 2], v[height // 2 :])


def sides(side, mine_ref, recv_ref, offset, height):
    mine = rows_of(side, mine_ref, offset, height)
    recv = rows_of(side, recv_ref, offset, height)
    return jnp.where(side == 0, mine, recv), jnp.where(side == 0, recv, mine)


def close_trans_kernel(tall, long, flat, side_ref, a_ref, b_ref, ra_ref, rb_ref, expand_ref, contract_ref, cond_ref):
    side = side_ref[0]
    for t in range(4):
        refs = (a_ref, ra_ref, t * tall) if t < 3 else (b_ref, rb_ref, 0)
        low, high = sides(side, *refs, tall)
        expand_ref[:, 0, t * TILE : (t + 1) * TILE] = low
        expand_ref[:, 1, t * TILE : (t + 1) * TILE] = high
    low, high = sides(side, b_ref, rb_ref, tall, long)
    contract_ref[:, :TILE] = low
    contract_ref[:, TILE:] = high
    low, high = sides(side, a_ref, ra_ref, 3 * tall, flat)
    cond_ref[0, :, :TILE] = low
    cond_ref[1, :, :TILE] = high
    low, high = sides(side, b_ref, rb_ref, tall + long, flat)
    cond_ref[0, :, TILE:] = low
    cond_ref[1, :, TILE:] = high
    low, high = sides(side, b_ref, rb_ref, tall + long + flat, flat)
    cond_ref[2, :, :TILE] = low
    cond_ref[2, :, TILE:] = high


def close_attn_kernel(tall, flat, side_ref, a_ref, b_ref, ra_ref, rb_ref, cond_in, attn_ref, out_ref, cond_ref):
    side = side_ref[0]
    for t in range(4):
        refs = (a_ref, ra_ref, t * tall) if t < 3 else (b_ref, rb_ref, 0)
        low, high = sides(side, *refs, tall)
        cut = slice((t % 2) * TILE, (t % 2 + 1) * TILE)
        attn_ref[:, t // 2, cut] = low
        attn_ref[:, 2 + t // 2, cut] = high
    low, high = sides(side, b_ref, rb_ref, tall, tall)
    out_ref[:, :TILE] = low
    out_ref[:, TILE:] = high
    for t in range(2):
        low, high = sides(side, b_ref, rb_ref, 2 * tall + t * flat, flat)
        cond_ref[:, 0, t * TILE : (t + 1) * TILE] = low
        cond_ref[:, 1, t * TILE : (t + 1) * TILE] = high
    low, high = sides(side, b_ref, rb_ref, 2 * tall + 2 * flat, flat)
    cond_ref[:, 2, :TILE] = low
    cond_ref[:, 2, TILE:] = high
    for k in range(3):
        cond_ref[:, 3 + k, :] = cond_in[k]


def close(kernel, side, operands, shapes, name):
    vm = pl.BlockSpec(memory_space=pltpu.VMEM)
    return pl.pallas_call(
        kernel,
        in_specs=[pl.BlockSpec(memory_space=pltpu.SMEM)] + [vm] * len(operands),
        out_specs=[vm] * len(shapes),
        out_shape=[jax.ShapeDtypeStruct(shape, F32) for shape in shapes],
        cost_estimate=pl.CostEstimate(flops=0, transcendentals=0, bytes_accessed=4 << 20),
        name=name,
    )(side, *operands)


def tie(*values):
    return lax.optimization_barrier(values)


def body(
    single,
    conditioning,
    pair_features,
    segments,
    pad_mask,
    cotangent,
    cond_gain,
    cond_weight,
    biases,
    attn_weight,
    out_weight,
    pair_gain,
    pair_weight,
    expand_weight,
    contract_weight,
):
    rows, width = single.shape
    cond_width = conditioning.shape[1]
    heads = pair_weight.shape[1]
    hidden_width = contract_weight.shape[0]
    crops = lax.axis_size("crop")
    bits = crops.bit_length() - 1
    me = lax.axis_index("crop").astype(jnp.int32).reshape(1)
    side = lax.axis_index("seq").astype(jnp.int32).reshape(1)
    orders = (tuple(range(bits)), (1, 0) + tuple(range(2, bits)))
    gains = cond_gain.T
    cond_weights = cond_weight.transpose(1, 0, 2)
    attn_weights = attn_weight.transpose(1, 0, 2)
    expand_weights = expand_weight.transpose(1, 0, 2)
    pair = pair_features[0]
    own_segments = lax.dynamic_slice(segments[0], (side[0] * rows,), (rows,))[:, None]

    x, queries, kv, scale0, scale1, keep0, keep1, w_forward, w_backward = front(
        single, conditioning, gains, biases.T, pair_gain[None], pair_weight.T, cond_weights, attn_weights
    )
    kv_other = swap(kv)
    x_other = swap(x)
    own_t, send_t, kept, grad_norm1, grad_cond1, direct1, sums1, gain_sum1 = trans(
        side, x, single, conditioning, cotangent, gains, scale1, keep1, expand_weights, contract_weight, cond_weights
    )
    recv_t = swap(send_t)
    gate, grad_mixed, grad_attended = middle(x, cotangent, keep0, attn_weights, out_weight)

    tall, flat, long = width // crops, cond_width // crops, hidden_width // crops
    plan_t, totals_t = layout(
        (
            (0, width, width, (0, 0, 0, 1)),
            (1, 0, hidden_width, (1,)),
            (0, 2 * width + cond_width, cond_width, (0, 1)),
            (0, 2 * width + 2 * cond_width, cond_width, (1,)),
        ),
        crops,
        hidden_width,
    )
    keep_a, send_a, keep_b, send_b = wgrad(me, x, x_other, own_t, recv_t, plan_t, orders, totals_t, "wgrad_trans")
    w_forward, grad_attended, keep_a, send_a, keep_b, send_b = tie(
        w_forward, grad_attended, keep_a, send_a, keep_b, send_b
    )
    state_t = [(keep_a, send_a), (keep_b, send_b)]
    arrived = arrivals(state_t, 0, orders)
    bias, inv, mean = pair_fwd(pair, w_forward, heads)
    bias, kv_other, arrived = tie(bias, kv_other, arrived)
    state_t = added(state_t, arrived)
    bias, state_t = tie(bias, state_t)

    arrived = arrivals(state_t, 1, orders)
    attended, grad_queries, dkv_own, dkv_send, r, t, s = attention(
        side, queries, kv, kv_other, grad_attended, bias, inv, mean, own_segments, segments, pad_mask
    )
    dkv_send, arrived = tie(dkv_send, arrived)
    dkv_recv = swap(dkv_send)
    state_t = added(state_t, arrived)
    dkv_recv, state_t = tie(dkv_recv, state_t)

    arrived = arrivals(state_t, 2, orders)
    own_a, sent_a, layer_out, grad_single, grad_cond, sums0, gain_sum0 = after(
        side, x, single, conditioning, cotangent, gains, scale0, keep0, gate, grad_mixed, attended, grad_queries,
        dkv_own, dkv_recv, kept, grad_norm1, grad_cond1, direct1, attn_weights, out_weight, cond_weights,
    )
    sent_a, arrived = tie(sent_a, arrived)
    recv_a = swap(sent_a)
    state_t = added(state_t, arrived)
    recv_a, state_t = tie(recv_a, state_t)
    plan_a, totals_a = layout(
        (
            (0, 0, width, (0, 0, 0, 1)),
            (1, 0, width, (1,)),
            (0, 2 * width, cond_width, (1, 1)),
            (0, 2 * width + 2 * cond_width, cond_width, (1,)),
        ),
        crops,
        width,
    )
    keep_a, send_a, keep_b, send_b = wgrad(me, x, x_other, own_a, recv_a, plan_a, orders, totals_a, "wgrad_attn")
    r, keep_a, send_a, keep_b, send_b = tie(r, keep_a, send_a, keep_b, send_b)
    state_a = [(keep_a, send_a), (keep_b, send_b)]

    arrived_a = arrivals(state_a, 0, orders)
    arrived = arrivals(state_t, 3, orders)
    grad_pair, n_sum, c_sum = pair_bwd(pair, r, t, s, mean, w_backward)
    n_sum, c_sum, arrived, arrived_a = tie(n_sum, c_sum, arrived, arrived_a)
    state_a = added(state_a, arrived_a)
    state_t = added(state_t, arrived)
    for j in range(4, bits):
        state_t = added(state_t, arrivals(state_t, j, orders))
    n_sum, state_a, state_t = tie(n_sum, state_a, state_t)

    normed = n_sum - jnp.sum(c_sum, axis=1, keepdims=True)
    grad_pair_weight = (normed * pair_gain.astype(F32)[None]).T
    grad_pair_gain = jnp.sum(pair_weight.astype(F32).T * normed, axis=0)
    devices = 2 * crops

    def tiles(v, lanes):
        count = v.shape[0]
        v = v.reshape(count, devices, -1).transpose(1, 0, 2)
        return jnp.pad(v, ((0, 0), (0, 8 - count), (0, lanes - v.shape[2])))

    chan_part = pair_gain.shape[0] // devices
    weight_tile = jnp.pad(
        grad_pair_weight.reshape(devices, chan_part, heads), ((0, 0), (0, 8 - chan_part), (0, 32 - heads))
    )
    small = jnp.concatenate(
        [
            tiles(jnp.concatenate([sums0[:2], sums1, sums0[2:]]), 32),
            tiles(jnp.concatenate([gain_sum0, gain_sum1]), 32),
            tiles(grad_pair_gain[None], 32),
            weight_tile,
        ],
        axis=2,
    ).reshape(crops, 2, 8, 128)
    wanted = jnp.stack([me[0] ^ place(p, orders[0]) for p in range(crops)])
    small = jnp.take(small, wanted, axis=0)
    state_s = [(small[: crops // 2], small[crops // 2 :])]
    trans_a, trans_b = state_t[0][0], state_t[1][0]
    arrived_a = arrivals(state_a, 1, orders)
    arrived_s = arrivals(state_s, 0, orders[:1])
    grad_expand, grad_contract, cond1 = close(
        functools.partial(close_trans_kernel, tall, long, flat),
        side,
        (trans_a, trans_b, swap(trans_a), swap(trans_b)),
        ((tall // 2, 2, hidden_width), (long // 2, width), (3, flat // 2, width)),
        "close_trans",
    )
    cond1, arrived_a, arrived_s = tie(cond1, arrived_a, arrived_s)
    state_a, state_s = added(state_a, arrived_a), added(state_s, arrived_s)
    for j in range(2, bits):
        state_a, state_s = tie(state_a, state_s)
        arrived_a, arrived_s = arrivals(state_a, j, orders), arrivals(state_s, j - 1, orders[:1])
        arrived_a, arrived_s = tie(arrived_a, arrived_s)
        state_a, state_s = added(state_a, arrived_a), added(state_s, arrived_s)
    state_a, state_s = tie(state_a, state_s)
    attn_a, attn_b = state_a[0][0], state_a[1][0]
    attn_ra, attn_rb = swap(attn_a), swap(attn_b)
    small = added(state_s, arrivals(state_s, bits - 1, orders[:1]))[0][0]
    grad_attn_weight, grad_out, grad_cond_weight = close(
        functools.partial(close_attn_kernel, tall, flat),
        side,
        (attn_a, attn_b, attn_ra, attn_rb, cond1),
        ((tall // 2, 4, width), (tall // 2, width), (flat // 2, 6, width)),
        "close_attn",
    )
    low, high = small[0], small[1]
    small = jnp.where(side[0] == 0, low, high) + swap(jnp.where(side[0] == 0, high, low))
    return (
        layer_out,
        grad_single,
        grad_cond,
        grad_pair[None],
        small[:2, 32 : 32 + cond_width // devices].T,
        grad_cond_weight,
        small[:5, : width // devices].T,
        grad_attn_weight,
        grad_out,
        small[0, 64 : 64 + chan_part],
        small[:chan_part, 96 : 96 + heads],
        grad_expand,
        grad_contract,
    )


def solution(mesh):
    token = P(("crop", "seq"), None)
    whole = P()
    cube = P(("crop", "seq"), None, None)
    return jax.shard_map(
        body,
        mesh=mesh,
        in_specs=(token, token, P("crop", "seq", None, None), P("crop", None), P("crop", None), token)
        + (whole,) * 9,
        out_specs=(
            token, token, token, P("crop", "seq", None, None), token, cube, token, cube, token,
            P(("crop", "seq")), token, cube, token,
        ),
        check_vma=False,
    )
```

```python
import functools
import math
import jax
import jax.numpy as jnp
from jax import lax
from jax.experimental import pallas as pl
from jax.experimental.pallas import tpu as pltpu
from jax.sharding import PartitionSpec as P

EPS = 1e-05
NEG = -1e30
F32 = jnp.float32
BF16 = jnp.bfloat16


def dot_nt(a, b):
    return lax.dot_general(a, b, (((1,), (1,)), ((), ())), preferred_element_type=F32)


def dot_tn(a, b):
    return lax.dot_general(a, b, (((0,), (0,)), ((), ())), preferred_element_type=F32)


def dot_nn(a, b):
    return jnp.dot(a, b, preferred_element_type=F32)


def split3(v):
    hi = v.astype(BF16)
    rest = v - hi.astype(F32)
    mid = rest.astype(BF16)
    lo = (rest - mid.astype(F32)).astype(BF16)
    return hi, mid, lo


def pair_fwd_kernel(x_ref, w_ref, bias_ref, inv_ref, mean_ref):
    rows, keys, chan = x_ref.shape
    heads = bias_ref.shape[0]
    w = w_ref[...]
    ones = jnp.full((8, chan), 1.0, BF16)
    for base in range(0, rows, 8):
        parts = []
        invs = []
        means = []
        for i in range(base, base + 8):
            x = x_ref[i]
            raw = dot_nt(w, x)
            mean = raw[3 * heads : 3 * heads + 1] * (1.0 / chan)
            wide = x.astype(F32)
            centred = wide - jnp.mean(wide, axis=-1, keepdims=True)
            square = (centred * centred).astype(BF16)
            var = dot_nt(ones, square)[0:1] * (1.0 / chan)
            inv = lax.rsqrt(var + EPS)
            parts.append((raw[:heads] + raw[heads : 2 * heads] + raw[2 * heads : 3 * heads]) * inv)
            invs.append(inv)
            means.append(mean)
        block = jnp.stack(parts, axis=0)
        bias_ref[:, base : base + 8, :] = pltpu.einshape("ihj->hij", block).astype(BF16)
        inv_ref[base : base + 8, :] = jnp.concatenate(invs, axis=0)
        mean_ref[base : base + 8, :] = jnp.concatenate(means, axis=0)


def pair_fwd(x, w, heads, tile=32):
    rows, keys, chan = x.shape
    return pl.pallas_call(
        pair_fwd_kernel,
        grid=(rows // tile,),
        in_specs=[
            pl.BlockSpec((tile, keys, chan), lambda i: (i, 0, 0)),
            pl.BlockSpec(w.shape, lambda i: (0, 0)),
        ],
        out_specs=[
            pl.BlockSpec((heads, tile, keys), lambda i: (0, i, 0)),
            pl.BlockSpec((tile, keys), lambda i: (i, 0)),
            pl.BlockSpec((tile, keys), lambda i: (i, 0)),
        ],
        out_shape=[
            jax.ShapeDtypeStruct((heads, rows, keys), BF16),
            jax.ShapeDtypeStruct((rows, keys), F32),
            jax.ShapeDtypeStruct((rows, keys), F32),
        ],
        cost_estimate=pl.CostEstimate(flops=0, transcendentals=0, bytes_accessed=96 << 20),
        name="pair_fwd",
    )(x, w)


def attn_kernel(
    half_ref, q_ref, ko_ref, vo_ref, kr_ref, vr_ref, ga_ref, bias_ref, inv_ref, mean_ref, segc_ref, segr_ref, padr_ref,
    att_ref, dq_ref, own_ref, send_ref, r_ref, t_ref, s_ref,
    k_sc, v_sc, mask_sc, dk_sc, dv_sc, m2_sc,
):
    rows = q_ref.shape[0]
    heads, _, keys = bias_ref.shape
    size = q_ref.shape[1] // heads
    scale = 1.0 / math.sqrt(size)
    half = half_ref[0]
    own = pl.ds(pl.multiple_of(half * rows, 32), rows)
    other = pl.ds(pl.multiple_of((1 - half) * rows, 32), rows)
    k_sc[own, :] = ko_ref[...]
    k_sc[other, :] = kr_ref[...]
    v_sc[own, :] = vo_ref[...]
    v_sc[other, :] = vr_ref[...]

    @pl.when(pl.program_id(0) == 0)
    def _():
        row_id = lax.broadcasted_iota(jnp.int32, (rows, keys), 0) + half * rows
        col_id = lax.broadcasted_iota(jnp.int32, (rows, keys), 1)
        allowed = (segc_ref[...] == segr_ref[...]) & ((padr_ref[...] == 1) | (row_id == col_id))
        mask_sc[...] = jnp.where(allowed, 0.0, NEG)
        m2_sc[...] = jnp.zeros_like(m2_sc)

    inv = inv_ref[...]
    m2 = m2_sc[...]
    for h in range(heads):
        cut = slice(h * size, (h + 1) * size)
        qh = q_ref[:, cut]
        kh = k_sc[:, cut]
        vh = v_sc[:, cut]
        gh = ga_ref[:, cut]
        bias = bias_ref[h].astype(F32)
        scores = dot_nt(qh, kh) * scale + bias + mask_sc[...]
        top = jnp.max(scores, axis=-1, keepdims=True)
        e = jnp.exp(scores - top)
        p = e * (1.0 / jnp.sum(e, axis=-1, keepdims=True))
        low = p.astype(BF16)
        att_ref[:, cut] = dot_nn(low, vh).astype(BF16)
        gp = dot_nt(gh, vh)
        pg = p * gp
        delta = jnp.sum(pg, axis=-1, keepdims=True)
        gs32 = pg - p * delta
        gs = gs32.astype(BF16)
        dq_ref[:, cut] = (dot_nn(gs, kh) * scale).astype(BF16)
        dk_sc[:, cut] = dot_tn(gs, qh) * scale
        dv_sc[:, cut] = dot_tn(low, gh)
        m2 = m2 + gs32 * bias
        r_ref[h] = (gs.astype(F32) * inv).astype(BF16)
    m2_sc[...] = m2
    own_ref[0] = dk_sc[own, :]
    own_ref[1] = dv_sc[own, :]
    send_ref[0] = dk_sc[other, :]
    send_ref[1] = dv_sc[other, :]

    @pl.when(pl.program_id(0) == pl.num_programs(0) - 1)
    def _():
        slope = inv * inv * m2 * (1.0 / 128.0)
        s_ref[...] = -slope
        t_ref[...] = slope * mean_ref[...]


def attention(half, q, kv, kv_other, ga, bias, inv, mean, segc, segr, padr):
    rows, width = q.shape
    heads, _, keys = bias.shape
    groups = 2
    part = width // groups

    def lanes(first):
        return pl.BlockSpec((rows, part), lambda g: (0, first + g))

    def fixed(shape):
        return pl.BlockSpec(shape, lambda g: (0,) * len(shape))

    plane = fixed((rows, keys))
    pair = pl.BlockSpec((2, rows, part), lambda g: (0, 0, g))
    head = pl.BlockSpec((heads // groups, rows, keys), lambda g: (g, 0, 0))
    return pl.pallas_call(
        attn_kernel,
        grid=(groups,),
        in_specs=[
            pl.BlockSpec(memory_space=pltpu.SMEM),
            lanes(0), lanes(0), lanes(groups), lanes(0), lanes(groups), lanes(0), head, plane, plane,
            fixed(segc.shape), fixed(segr.shape), fixed(padr.shape),
        ],
        out_specs=[lanes(0), lanes(0), pair, pair, head, plane, plane],
        out_shape=[
            jax.ShapeDtypeStruct((rows, width), BF16),
            jax.ShapeDtypeStruct((rows, width), BF16),
            jax.ShapeDtypeStruct((2, rows, width), F32),
            jax.ShapeDtypeStruct((2, rows, width), F32),
            jax.ShapeDtypeStruct((heads, rows, keys), BF16),
            jax.ShapeDtypeStruct((rows, keys), F32),
            jax.ShapeDtypeStruct((rows, keys), F32),
        ],
        scratch_shapes=[
            pltpu.VMEM((keys, part), BF16),
            pltpu.VMEM((keys, part), BF16),
            pltpu.VMEM((rows, keys), F32),
            pltpu.VMEM((keys, part), F32),
            pltpu.VMEM((keys, part), F32),
            pltpu.VMEM((rows, keys), F32),
        ],
        cost_estimate=pl.CostEstimate(flops=0, transcendentals=0, bytes_accessed=60 << 20),
        name="attn",
    )(half, q, kv, kv, kv_other, kv_other, ga, bias, inv, mean, segc, segr, padr)


def pair_bwd_kernel(x_ref, r_ref, t_ref, s_ref, mean_ref, w_ref, out_ref, n_ref, c_ref):
    rows, keys, chan = x_ref.shape
    heads = r_ref.shape[0]
    depth = w_ref.shape[0]
    w = w_ref[...]

    @pl.when(pl.program_id(0) == 0)
    def _():
        n_ref[...] = jnp.zeros_like(n_ref)
        c_ref[...] = jnp.zeros_like(c_ref)

    acc = jnp.zeros(n_ref.shape, F32)
    corr = jnp.zeros(c_ref.shape, F32)
    pad = jnp.zeros((depth - 2 * heads - 6, keys), F32)
    for base in range(0, rows, 8):
        block = pltpu.einshape("hij->ihj", r_ref[:, base : base + 8, :].astype(F32))
        for k in range(8):
            i = base + k
            r32 = block[k]
            t = t_ref[i : i + 1, :]
            s = s_ref[i : i + 1, :]
            th, tm, tl = (v.astype(F32) for v in split3(t))
            sh, sm, sl = (v.astype(F32) for v in split3(s))
            left = jnp.concatenate([r32, r32, th, tm, tl, sh, sm, sl, pad], axis=0).astype(BF16)
            both = dot_tn(left, w)
            x = x_ref[i]
            out_ref[i] = (both[:, :chan] + x.astype(F32) * both[:, chan:]).astype(BF16)
            acc = acc + dot_nn(r32.astype(BF16), x)
            corr = corr + r32 * mean_ref[i : i + 1, :]
    n_ref[...] += acc
    c_ref[...] += corr


def pair_bwd(x, r, t, s, mean, w, tile=32):
    rows, keys, chan = x.shape
    heads = r.shape[0]
    return pl.pallas_call(
        pair_bwd_kernel,
        grid=(rows // tile,),
        in_specs=[
            pl.BlockSpec((tile, keys, chan), lambda i: (i, 0, 0)),
            pl.BlockSpec((heads, tile, keys), lambda i: (0, i, 0)),
            pl.BlockSpec((tile, keys), lambda i: (i, 0)),
            pl.BlockSpec((tile, keys), lambda i: (i, 0)),
            pl.BlockSpec((tile, keys), lambda i: (i, 0)),
            pl.BlockSpec(w.shape, lambda i: (0, 0)),
        ],
        out_specs=[
            pl.BlockSpec((tile, keys, chan), lambda i: (i, 0, 0)),
            pl.BlockSpec((heads, chan), lambda i: (0, 0)),
            pl.BlockSpec((heads, keys), lambda i: (0, 0)),
        ],
        out_shape=[
            jax.ShapeDtypeStruct((rows, keys, chan), BF16),
            jax.ShapeDtypeStruct((heads, chan), F32),
            jax.ShapeDtypeStruct((heads, keys), F32),
        ],
        cost_estimate=pl.CostEstimate(flops=0, transcendentals=0, bytes_accessed=60 << 20),
        name="pair_bwd",
    )(x, r, t, s, mean, w)


def norm_rows(values):
    centred = values - jnp.mean(values, -1, keepdims=True)
    inverse = lax.rsqrt(jnp.mean(centred * centred, -1, keepdims=True) + EPS)
    return (centred * inverse, inverse)


def norm_back(incoming, normal, inverse):
    return inverse * (
        incoming
        - jnp.mean(incoming, -1, keepdims=True)
        - normal * jnp.mean(incoming * normal, -1, keepdims=True)
    )


def sigmoid(v):
    return jax.nn.sigmoid(v)


def fetch(pairs, sems):
    copies = [pltpu.make_async_copy(src, dst, sems.at[k]) for k, (src, dst) in enumerate(pairs)]
    for copy in copies:
        copy.start()
    return copies


def put(side, own_ref, send_ref, start, low, high):
    stop = start + low.shape[1]

    @pl.when(side == 0)
    def _():
        own_ref[:, start:stop] = low
        send_ref[:, start:stop] = high

    @pl.when(side != 0)
    def _():
        own_ref[:, start:stop] = high
        send_ref[:, start:stop] = low


def total(v):
    return jnp.sum(v.astype(F32), axis=0, keepdims=True)


def pair_weights(gain_ref, weight_ref, forward_ref, backward_ref):
    gained = weight_ref[...].astype(F32) * gain_ref[...].astype(F32)
    heads, chan = gained.shape
    hi, mid, lo = split3(gained - jnp.mean(gained, axis=1, keepdims=True))
    forward_ref[0:heads, :] = hi
    forward_ref[heads : 2 * heads, :] = mid
    forward_ref[2 * heads : 3 * heads, :] = lo
    row = lax.broadcasted_iota(jnp.int32, (16, chan), 0)
    forward_ref[3 * heads :, :] = jnp.where(row == 0, 1.0, 0.0).astype(BF16)
    backward_ref[0:heads, :chan] = hi
    backward_ref[heads : 2 * heads, :chan] = mid
    backward_ref[0 : 2 * heads, chan:] = jnp.zeros((2 * heads, chan), BF16)
    backward_ref[2 * heads :, :chan] = jnp.where(row < 3, 1.0, 0.0).astype(BF16)
    backward_ref[2 * heads :, chan:] = jnp.where((row >= 3) & (row < 6), 1.0, 0.0).astype(BF16)


def trans_kernel(
    side_ref, single_ref, cond_ref, cot_ref, gain_ref, bias_ref, pair_gain_ref, pair_weight_ref, cw_hbm, ew_hbm, tw_hbm,
    x_hbm, scale0_hbm, keep0_hbm,
    own_ref, send_ref, kept_ref, grad_norm_ref, grad_cond_ref, grad_direct_ref, sums_ref, gain_sum_ref,
    forward_ref, backward_ref,
    cw, ew, tw, x_ref, scale0_ref, keep0_ref, scale1_ref, sems, out_sems,
):
    order = (3, 4, 5, 0, 1, 2)
    copies = fetch(
        [(cw_hbm.at[k], cw.at[k]) for k in order[:3]]
        + [(ew_hbm.at[0], ew.at[0]), (ew_hbm.at[1], ew.at[1]), (tw_hbm, tw)]
        + [(cw_hbm.at[k], cw.at[k]) for k in order[3:]],
        sems,
    )
    side = side_ref[0]
    rows, width = single_ref.shape
    cond_width = cond_ref.shape[1]
    cut = width // 2
    hidden_width = tw.shape[0]
    pair_weights(pair_gain_ref, pair_weight_ref, forward_ref, backward_ref)
    single_norm, _ = norm_rows(single_ref[...].astype(F32))
    cond_norm, _ = norm_rows(cond_ref[...].astype(F32))
    cond = cond_ref[...]
    x_ref[:, 2 * width + 2 * cond_width :] = cond

    def modulate(b, waits, scale_ref):
        low = (cond_norm * gain_ref[b : b + 1, :].astype(F32)).astype(BF16)
        x_ref[:, 2 * width + b * cond_width : 2 * width + (b + 1) * cond_width] = low
        waits[0].wait()
        scale = sigmoid(dot_nn(low, cw[3 * b]) + bias_ref[2 * b : 2 * b + 1, :].astype(F32))
        scale_ref[...] = scale
        waits[1].wait()
        shift = dot_nn(low, cw[3 * b + 1])
        x_ref[:, b * width : (b + 1) * width] = (scale * single_norm + shift).astype(BF16)
        waits[2].wait()
        return sigmoid(dot_nn(cond, cw[3 * b + 2]) + bias_ref[2 * b + 1 : 2 * b + 2, :].astype(F32))

    keep = modulate(1, copies[:3], scale1_ref)
    keep0_ref[...] = modulate(0, copies[6:], scale0_ref)
    leaving = fetch([(x_ref, x_hbm), (scale0_ref, scale0_hbm), (keep0_ref, keep0_hbm)], out_sems)
    trans_in = x_ref[:, width : 2 * width]
    upstream = cot_ref[...].astype(F32)
    grad_trans = (upstream * keep).astype(BF16)
    at = hidden_width
    put(side, own_ref, send_ref, at + hidden_width, grad_trans[:, :cut], grad_trans[:, cut:])
    for copy in copies[3:6]:
        copy.wait()
    grad_in = jnp.zeros((rows, width), F32)
    trans_out = jnp.zeros((rows, width), F32)
    step = 512
    for c in range(0, hidden_width, step):
        span = slice(c, c + step)
        gate_pre = dot_nn(trans_in, ew[0, :, span])
        up_pre = dot_nn(trans_in, ew[1, :, span])
        sig = sigmoid(gate_pre)
        act = gate_pre * sig
        hidden = (act * up_pre).astype(BF16)
        own_ref[:, span] = hidden
        send_ref[:, span] = hidden
        trans_out = trans_out + dot_nn(hidden, tw[span, :])
        grad_hidden = dot_nt(grad_trans, tw[span, :])
        grad_gate = (grad_hidden * up_pre * sig * (1.0 + gate_pre * (1.0 - sig))).astype(BF16)
        grad_up = (grad_hidden * act).astype(BF16)
        put(side, own_ref, send_ref, at + c, grad_gate, grad_up)
        grad_in = grad_in + dot_nt(grad_gate, ew[0, :, span]) + dot_nt(grad_up, ew[1, :, span])
    kept_ref[...] = keep * trans_out
    grad_keep = (upstream * trans_out * keep * (1.0 - keep)).astype(BF16)
    finish_branch(
        side, 1, 2 * hidden_width + cut, (), cw.at[3:6], single_ref, cond_ref, gain_ref, scale1_ref, grad_in, grad_keep,
        own_ref, send_ref, grad_norm_ref, grad_cond_ref, grad_direct_ref, sums_ref, gain_sum_ref,
    )
    for copy in leaving:
        copy.wait()


def trans(side, single, cond, cot, gains, biases, pair_gain, pair_weight, cw, ew, tw):
    rows, width = single.shape
    cond_width = cond.shape[1]
    hidden_width = tw.shape[0]
    heads, chan = pair_weight.shape
    packed = 2 * hidden_width + width // 2 + width + width // 2
    x_width = 2 * width + 3 * cond_width
    vm = pl.BlockSpec(memory_space=pltpu.VMEM)
    hbm = pl.BlockSpec(memory_space=pl.ANY)
    wide = jax.ShapeDtypeStruct((rows, width), F32)
    narrow = jax.ShapeDtypeStruct((rows, cond_width), F32)
    return pl.pallas_call(
        trans_kernel,
        in_specs=[pl.BlockSpec(memory_space=pltpu.SMEM)] + [vm] * 7 + [hbm] * 3,
        out_specs=[hbm] * 3 + [vm] * 10,
        out_shape=[
            jax.ShapeDtypeStruct((rows, x_width), BF16),
            wide,
            wide,
            jax.ShapeDtypeStruct((rows, packed), BF16),
            jax.ShapeDtypeStruct((rows, packed), BF16),
            wide,
            wide,
            narrow,
            narrow,
            jax.ShapeDtypeStruct((2, width), F32),
            jax.ShapeDtypeStruct((1, cond_width), F32),
            jax.ShapeDtypeStruct((3 * heads + 16, chan), BF16),
            jax.ShapeDtypeStruct((2 * heads + 16, 2 * chan), BF16),
        ],
        scratch_shapes=[
            pltpu.VMEM(cw.shape, BF16),
            pltpu.VMEM(ew.shape, BF16),
            pltpu.VMEM(tw.shape, BF16),
            pltpu.VMEM((rows, x_width), BF16),
            pltpu.VMEM((rows, width), F32),
            pltpu.VMEM((rows, width), F32),
            pltpu.VMEM((rows, width), F32),
            pltpu.SemaphoreType.DMA((9,)),
            pltpu.SemaphoreType.DMA((3,)),
        ],
        cost_estimate=pl.CostEstimate(flops=0, transcendentals=0, bytes_accessed=50 << 20),
        name="trans",
    )(side, single, cond, cot, gains, biases, pair_gain, pair_weight, cw, ew, tw)


def finish_branch(
    side, b, at, copies, cw, single_ref, cond_ref, gain_ref, scale_ref, grad_in, grad_keep,
    own_ref, send_ref, grad_norm_ref, grad_cond_ref, grad_direct_ref, sums_ref, gain_sum_ref,
):
    width = single_ref.shape[1]
    cut = width // 2
    single_norm, _ = norm_rows(single_ref[...].astype(F32))
    cond_norm, _ = norm_rows(cond_ref[...].astype(F32))
    scale = scale_ref[...]
    grad_scale = (grad_in * single_norm * scale * (1.0 - scale)).astype(BF16)
    grad_shift = grad_in.astype(BF16)
    put(side, own_ref, send_ref, at, grad_scale, grad_shift)
    put(side, own_ref, send_ref, at + width, grad_keep[:, :cut], grad_keep[:, cut:])
    grad_norm_ref[...] = grad_in * scale
    for copy in copies:
        copy.wait()
    grad_low = dot_nt(grad_scale, cw[0]) + dot_nt(grad_shift, cw[1])
    grad_cond_ref[...] = grad_low * gain_ref[b : b + 1, :].astype(F32)
    grad_direct_ref[...] = dot_nt(grad_keep, cw[2])
    gain_sum_ref[...] = total(grad_low * cond_norm)
    sums_ref[0:1, :] = total(grad_scale)
    sums_ref[1:2, :] = total(grad_keep)


def project_kernel(
    x_hbm, cot_ref, bias_ref, keep_hbm, aw_hbm, ow_hbm, q_ref, kv_ref, gate_ref, mixed_ref, attended_ref,
    x, keep, aw, ow, sems,
):
    width = cot_ref.shape[1]
    copies = fetch(
        [(x_hbm.at[:, :width], x)] + [(aw_hbm.at[k], aw.at[k]) for k in range(4)] + [(keep_hbm, keep), (ow_hbm, ow)], sems
    )
    copies[0].wait()
    copies[1].wait()
    q_ref[...] = (dot_nn(x[...], aw[0]) + bias_ref[4:5, :].astype(F32)).astype(BF16)
    copies[2].wait()
    kv_ref[:, :width] = dot_nn(x[...], aw[1]).astype(BF16)
    copies[3].wait()
    kv_ref[:, width:] = dot_nn(x[...], aw[2]).astype(BF16)
    copies[4].wait()
    gate = sigmoid(dot_nn(x[...], aw[3]))
    gate_ref[...] = gate
    copies[5].wait()
    grad_attn = (cot_ref[...].astype(F32) * keep[...]).astype(BF16)
    copies[6].wait()
    grad_mixed = dot_nt(grad_attn, ow[...])
    mixed_ref[...] = grad_mixed
    attended_ref[...] = (grad_mixed * gate).astype(BF16)


def project(x, cot, biases, keep, aw, ow):
    rows, width = cot.shape
    vm = pl.BlockSpec(memory_space=pltpu.VMEM)
    hbm = pl.BlockSpec(memory_space=pl.ANY)
    return pl.pallas_call(
        project_kernel,
        in_specs=[hbm, vm, vm, hbm, hbm, hbm],
        out_specs=[vm] * 5,
        out_shape=[
            jax.ShapeDtypeStruct((rows, width), BF16),
            jax.ShapeDtypeStruct((rows, 2 * width), BF16),
            jax.ShapeDtypeStruct((rows, width), F32),
            jax.ShapeDtypeStruct((rows, width), F32),
            jax.ShapeDtypeStruct((rows, width), BF16),
        ],
        scratch_shapes=[
            pltpu.VMEM((rows, width), BF16),
            pltpu.VMEM((rows, width), F32),
            pltpu.VMEM(aw.shape, BF16),
            pltpu.VMEM(ow.shape, BF16),
            pltpu.SemaphoreType.DMA((7,)),
        ],
        cost_estimate=pl.CostEstimate(flops=0, transcendentals=0, bytes_accessed=22 << 20),
        name="project",
    )(x, cot, biases, keep, aw, ow)


def after_kernel(
    side_ref, single_ref, cond_ref, cot_ref, gain_ref,
    attended_hbm, gate_hbm, ow_hbm, keep_hbm, kept_hbm, grad_q_hbm, dkv_own_hbm, dkv_recv_hbm, grad_mixed_hbm, aw_hbm,
    scale_hbm, cw_hbm, grad_norm1_hbm, grad_cond1_hbm, direct1_hbm,
    own_ref, send_ref, layer_hbm, grad_single_ref, grad_cond_ref, sums_ref, gain_sum_ref,
    attended_ref, gate_ref, ow, keep_ref, kept_ref, grad_q_ref, dkv_own_ref, dkv_recv_ref, grad_mixed_ref, aw,
    scale_ref, cw, grad_norm1_ref, grad_cond1_ref, direct1_ref, layer_ref, norm_sc, cond_sc, direct_sc, sems, out_sem,
):
    sources = [
        (attended_hbm, attended_ref), (gate_hbm, gate_ref), (ow_hbm, ow), (keep_hbm, keep_ref), (kept_hbm, kept_ref),
        (grad_q_hbm, grad_q_ref), (dkv_own_hbm, dkv_own_ref), (dkv_recv_hbm, dkv_recv_ref),
        (grad_mixed_hbm, grad_mixed_ref),
    ]
    sources += [(aw_hbm.at[k], aw.at[k]) for k in range(4)]
    sources += [(scale_hbm, scale_ref)] + [(cw_hbm.at[k], cw.at[k]) for k in range(3)]
    sources += [(grad_norm1_hbm, grad_norm1_ref), (grad_cond1_hbm, grad_cond1_ref), (direct1_hbm, direct1_ref)]
    copies = fetch(sources, sems)
    side = side_ref[0]
    width = single_ref.shape[1]
    cut = width // 2
    upstream = cot_ref[...].astype(F32)
    single_norm, single_inverse = norm_rows(single_ref[...].astype(F32))
    cond_norm, cond_inverse = norm_rows(cond_ref[...].astype(F32))
    copies[0].wait()
    copies[1].wait()
    gate = gate_ref[...]
    attended = attended_ref[...].astype(F32)
    mixed = (attended * gate).astype(BF16)
    own_ref[:, :width] = mixed
    send_ref[:, :width] = mixed
    copies[2].wait()
    attn_out = dot_nn(mixed, ow[...])
    copies[3].wait()
    keep = keep_ref[...]
    copies[4].wait()
    layer_ref[...] = (single_ref[...].astype(F32) + keep * attn_out + kept_ref[...]).astype(BF16)
    leaving = pltpu.make_async_copy(layer_ref, layer_hbm, out_sem)
    leaving.start()
    grad_keep = (upstream * attn_out * keep * (1.0 - keep)).astype(BF16)
    grad_attn = (upstream * keep).astype(BF16)
    put(side, own_ref, send_ref, 3 * width, grad_attn[:, :cut], grad_attn[:, cut:])
    for copy in copies[5:9]:
        copy.wait()
    grad_q = grad_q_ref[...]
    grad_k = (dkv_own_ref[0] + dkv_recv_ref[0]).astype(BF16)
    grad_v = (dkv_own_ref[1] + dkv_recv_ref[1]).astype(BF16)
    grad_logit = (grad_mixed_ref[...] * attended * gate * (1.0 - gate)).astype(BF16)
    put(side, own_ref, send_ref, width, grad_q, grad_v)
    put(side, own_ref, send_ref, 2 * width, grad_k, grad_logit)
    sums_ref[2:3, :] = total(grad_q)
    grad_in = jnp.zeros(single_ref.shape, F32)
    for k, part in enumerate((grad_q, grad_k, grad_v, grad_logit)):
        copies[9 + k].wait()
        grad_in = grad_in + dot_nt(part, aw[k])
    copies[13].wait()
    finish_branch(
        side, 0, 3 * width + cut, copies[14:17], cw, single_ref, cond_ref, gain_ref, scale_ref, grad_in, grad_keep,
        own_ref, send_ref, norm_sc, cond_sc, direct_sc, sums_ref, gain_sum_ref,
    )
    for copy in copies[17:]:
        copy.wait()
    grad_single_ref[...] = upstream + norm_back(norm_sc[...] + grad_norm1_ref[...], single_norm, single_inverse)
    grad_cond_ref[...] = (
        norm_back(cond_sc[...] + grad_cond1_ref[...], cond_norm, cond_inverse) + (direct_sc[...] + direct1_ref[...])
    )
    leaving.wait()


def after(side, single, cond, cot, gains, attended, gate, ow, keep, kept, grad_q, dkv_own, dkv_recv, grad_mixed, aw,
          scale, cw, grad_norm1, grad_cond1, direct1):
    rows, width = single.shape
    cond_width = cond.shape[1]
    packed = 3 * width + width // 2 + width + width // 2
    vm = pl.BlockSpec(memory_space=pltpu.VMEM)
    hbm = pl.BlockSpec(memory_space=pl.ANY)
    moved = (attended, gate, ow, keep, kept, grad_q, dkv_own, dkv_recv, grad_mixed, aw, scale, cw,
             grad_norm1, grad_cond1, direct1)
    shapes = [(3,) + v.shape[1:] if v is cw else v.shape for v in moved]
    return pl.pallas_call(
        after_kernel,
        in_specs=[pl.BlockSpec(memory_space=pltpu.SMEM)] + [vm] * 4 + [hbm] * len(moved),
        out_specs=[vm, vm, hbm] + [vm] * 4,
        out_shape=[
            jax.ShapeDtypeStruct((rows, packed), BF16),
            jax.ShapeDtypeStruct((rows, packed), BF16),
            jax.ShapeDtypeStruct((rows, width), BF16),
            jax.ShapeDtypeStruct((rows, width), F32),
            jax.ShapeDtypeStruct((rows, cond_width), F32),
            jax.ShapeDtypeStruct((3, width), F32),
            jax.ShapeDtypeStruct((1, cond_width), F32),
        ],
        scratch_shapes=[pltpu.VMEM(shape, v.dtype) for shape, v in zip(shapes, moved)]
        + [
            pltpu.VMEM((rows, width), BF16),
            pltpu.VMEM((rows, width), F32),
            pltpu.VMEM((rows, cond_width), F32),
            pltpu.VMEM((rows, cond_width), F32),
            pltpu.SemaphoreType.DMA((20,)),
            pltpu.SemaphoreType.DMA,
        ],
        cost_estimate=pl.CostEstimate(flops=0, transcendentals=0, bytes_accessed=40 << 20),
        name="after",
    )(side, single, cond, cot, gains, *moved)


TILE = 384


def place(position, order):
    count = len(order)
    return sum(((position >> (count - 1 - j)) & 1) << order[j] for j in range(count))


def wgrad_kernel(plan, orders, me_ref, *refs):
    sources, outs = refs[:4], refs[4:8]
    (x_own, x_recv, g_own, g_recv), turned_ref, results, sems, out_sems = refs[8:12], refs[12], refs[13:17], refs[17], refs[18]
    copies = fetch(list(zip(sources, (x_own, x_recv, g_own, g_recv))), sems)
    copies[0].wait()
    copies[1].wait()
    me = me_ref[0]
    blocks = 1 << len(orders[0])
    last = [max(k for k, group in enumerate(plan) if any(use[1] == color for use in group[3])) for color in (0, 1)]
    leaving = []
    for k, (source, start, width, uses) in enumerate(plan):
        height = width // blocks
        own, recv = ((x_own, x_recv), (g_own, g_recv))[source]
        span = slice(start, start + width)
        turned_ref[:width, :] = jnp.concatenate([own[:, span], recv[:, span]], axis=0).astype(F32).T
        if k == 0:
            copies[2].wait()
            copies[3].wait()
        for color in (0, 1):
            mine = [use for use in uses if use[1] == color]
            if mine:
                left = jnp.concatenate(
                    [
                        turned_ref[pl.ds(pl.multiple_of((me ^ place(p, orders[color])) * height, 8), height), :]
                        for p in range(blocks)
                    ],
                    axis=0,
                ).astype(BF16)
            keep_ref, send_ref = results[2 * color], results[2 * color + 1]
            for column, _, offset in mine:
                cut = slice(column, column + TILE)
                term = dot_nn(left, jnp.concatenate([g_own[:, cut], g_recv[:, cut]], axis=0)).astype(BF16)
                for p in range(blocks):
                    target = keep_ref if p < blocks // 2 else send_ref
                    target[p % (blocks // 2), offset : offset + height, :] = term[p * height : (p + 1) * height]
            if k == last[color]:
                for j in (2 * color, 2 * color + 1):
                    copy = pltpu.make_async_copy(results[j], outs[j], out_sems.at[j])
                    copy.start()
                    leaving.append(copy)
    for copy in leaving:
        copy.wait()


def wgrad(me, x_own, x_recv, g_own, g_recv, plan, orders, totals, name):
    rows = x_own.shape[0]
    blocks = 1 << len(orders[0])
    half = blocks // 2
    if any((width // blocks) % 8 for _, _, width, _ in plan):
        return wgrad_plain(me, x_own, x_recv, g_own, g_recv, plan, orders, totals)
    hbm = pl.BlockSpec(memory_space=pl.ANY)
    shapes = [(half, count, TILE) for count in totals for _ in range(2)]
    widest = max(group[2] for group in plan)
    moved = (x_own, x_recv, g_own, g_recv)
    return pl.pallas_call(
        functools.partial(wgrad_kernel, plan, orders),
        in_specs=[pl.BlockSpec(memory_space=pltpu.SMEM)] + [hbm] * 4,
        out_specs=[hbm] * 4,
        out_shape=[jax.ShapeDtypeStruct(shape, BF16) for shape in shapes],
        scratch_shapes=[pltpu.VMEM(v.shape, v.dtype) for v in moved]
        + [pltpu.VMEM((widest, 2 * rows), F32)]
        + [pltpu.VMEM(shape, BF16) for shape in shapes]
        + [pltpu.SemaphoreType.DMA((4,)), pltpu.SemaphoreType.DMA((4,))],
        cost_estimate=pl.CostEstimate(flops=0, transcendentals=0, bytes_accessed=26 << 20),
        name=name,
    )(me, *moved)


def wgrad_plain(me, x_own, x_recv, g_own, g_recv, plan, orders, totals):
    blocks = 1 << len(orders[0])
    pieces = ([], [])
    for source, start, width, uses in plan:
        own, recv = ((x_own, x_recv), (g_own, g_recv))[source]
        x = jnp.concatenate([own[:, start : start + width], recv[:, start : start + width]], axis=0)
        for column, color, offset in uses:
            g = jnp.concatenate([g_own[:, column : column + TILE], g_recv[:, column : column + TILE]], axis=0)
            wanted = jnp.stack([me[0] ^ place(p, orders[color]) for p in range(blocks)])
            term = jnp.take(dot_tn(x, g).reshape(blocks, width // blocks, TILE), wanted, axis=0)
            pieces[color].append((offset, term.astype(BF16)))
    outs = []
    for parts in pieces:
        whole = jnp.concatenate([term for _, term in sorted(parts, key=lambda part: part[0])], axis=1)
        outs += [whole[: blocks // 2], whole[blocks // 2 :]]
    return outs


def send_half(value, bit):
    count = lax.axis_size("crop")
    return lax.ppermute(value, "crop", [(i, i ^ (1 << bit)) for i in range(count)])


def arrivals(state, j, orders):
    return [send_half(send, order[j]) for (_, send), order in zip(state, orders)]


def add_kernel(*refs):
    if refs[0].shape[0] == 1 and len(refs) == 6:
        for color in (0, 1):
            refs[4 + color][...] = refs[2 * color][0].astype(F32) + refs[2 * color + 1][0].astype(F32)
        return
    for color in (0, 1):
        low, high, other_low, other_high = refs[4 * color : 4 * color + 4]
        keep, send = refs[8 + 2 * color : 10 + 2 * color]
        keep[...] = (low[...].astype(F32) + other_low[...].astype(F32)).astype(BF16)
        send[...] = (high[...].astype(F32) + other_high[...].astype(F32)).astype(BF16)


def added(state, arrived, name):
    count = state[0][0].shape[0]
    half = count // 2
    operands, in_specs, out_specs, out_shape = [], [], [], []
    for (keep, _), other in zip(state, arrived):
        block = (1,) + keep.shape[1:]
        if half:
            low = pl.BlockSpec(block, lambda p: (p, 0, 0))
            high = pl.BlockSpec(block, lambda p: (p + half, 0, 0))
            operands += [keep, keep, other, other]
            in_specs += [low, high, low, high]
            out_specs += [low, low]
            out_shape += [jax.ShapeDtypeStruct((half,) + keep.shape[1:], BF16)] * 2
        else:
            operands += [keep, other]
            in_specs += [pl.BlockSpec(memory_space=pltpu.VMEM)] * 2
            out_specs += [pl.BlockSpec(memory_space=pltpu.VMEM)]
            out_shape += [jax.ShapeDtypeStruct(keep.shape[1:], F32)]
    out = pl.pallas_call(
        add_kernel,
        grid=(half,) if half else (),
        in_specs=in_specs,
        out_specs=out_specs,
        out_shape=out_shape,
        cost_estimate=pl.CostEstimate(flops=0, transcendentals=0, bytes_accessed=2 << 20),
        name=name,
    )(*operands)
    return [(out[0], out[1]), (out[2], out[3])] if half else [(v, None) for v in out]


def swap(v):
    return lax.ppermute(v, "seq", [(0, 1), (1, 0)])


def rows_of(side, ref, offset, height):
    v = ref[offset : offset + height, :]
    return jnp.where(side == 0, v[: height // 2], v[height // 2 :])


def sides(side, mine_ref, recv_ref, offset, height):
    mine = rows_of(side, mine_ref, offset, height)
    recv = rows_of(side, recv_ref, offset, height)
    return jnp.where(side == 0, mine, recv), jnp.where(side == 0, recv, mine)


def close_trans_kernel(tall, long, flat, side_ref, a_ref, b_ref, ra_ref, rb_ref, expand_ref, contract_ref, cond_ref):
    side = side_ref[0]
    for t in range(4):
        refs = (a_ref, ra_ref, t * tall) if t < 3 else (b_ref, rb_ref, 0)
        low, high = sides(side, *refs, tall)
        expand_ref[:, 0, t * TILE : (t + 1) * TILE] = low
        expand_ref[:, 1, t * TILE : (t + 1) * TILE] = high
    low, high = sides(side, b_ref, rb_ref, tall, long)
    contract_ref[:, :TILE] = low
    contract_ref[:, TILE:] = high
    low, high = sides(side, a_ref, ra_ref, 3 * tall, flat)
    cond_ref[0, :, :TILE] = low
    cond_ref[1, :, :TILE] = high
    low, high = sides(side, b_ref, rb_ref, tall + long, flat)
    cond_ref[0, :, TILE:] = low
    cond_ref[1, :, TILE:] = high
    low, high = sides(side, b_ref, rb_ref, tall + long + flat, flat)
    cond_ref[2, :, :TILE] = low
    cond_ref[2, :, TILE:] = high


def close_attn_kernel(tall, flat, side_ref, a_ref, b_ref, ra_ref, rb_ref, cond_in, attn_ref, out_ref, cond_ref):
    side = side_ref[0]
    for t in range(4):
        refs = (a_ref, ra_ref, t * tall) if t < 3 else (b_ref, rb_ref, 0)
        low, high = sides(side, *refs, tall)
        cut = slice((t % 2) * TILE, (t % 2 + 1) * TILE)
        attn_ref[:, t // 2, cut] = low
        attn_ref[:, 2 + t // 2, cut] = high
    low, high = sides(side, b_ref, rb_ref, tall, tall)
    out_ref[:, :TILE] = low
    out_ref[:, TILE:] = high
    for t in range(2):
        low, high = sides(side, b_ref, rb_ref, 2 * tall + t * flat, flat)
        cond_ref[:, 0, t * TILE : (t + 1) * TILE] = low
        cond_ref[:, 1, t * TILE : (t + 1) * TILE] = high
    low, high = sides(side, b_ref, rb_ref, 2 * tall + 2 * flat, flat)
    cond_ref[:, 2, :TILE] = low
    cond_ref[:, 2, TILE:] = high
    for k in range(3):
        cond_ref[:, 3 + k, :] = cond_in[k]


def close(kernel, side, operands, shapes, name):
    vm = pl.BlockSpec(memory_space=pltpu.VMEM)
    return pl.pallas_call(
        kernel,
        in_specs=[pl.BlockSpec(memory_space=pltpu.SMEM)] + [vm] * len(operands),
        out_specs=[vm] * len(shapes),
        out_shape=[jax.ShapeDtypeStruct(shape, F32) for shape in shapes],
        cost_estimate=pl.CostEstimate(flops=0, transcendentals=0, bytes_accessed=4 << 20),
        name=name,
    )(side, *operands)


def small_kernel(
    groups, me_ref, sums0_ref, sums1_ref, gain0_ref, gain1_ref, n_ref, c_ref, pair_gain_ref, pair_weight_ref, *refs
):
    outs, tiles_ref = refs[:-1], refs[-1]
    devices = tiles_ref.shape[0]
    heads, chan = n_ref.shape
    normed = n_ref[...] - jnp.sum(c_ref[...], axis=1, keepdims=True)
    to_weight = (normed * pair_gain_ref[...].astype(F32)).T
    to_gain = total(pair_weight_ref[...].astype(F32) * normed)
    biases = jnp.concatenate([sums0_ref[0:2, :], sums1_ref[...], sums0_ref[2:3, :]], axis=0)
    gains = jnp.concatenate([gain0_ref[...], gain1_ref[...]], axis=0)
    wide, thin, part = biases.shape[1] // devices, gains.shape[1] // devices, chan // devices
    for d in range(devices):
        tiles_ref[d] = jnp.zeros(tiles_ref.shape[1:], F32)
        tiles_ref[d, 0:5, 0:wide] = biases[:, d * wide : (d + 1) * wide]
        tiles_ref[d, 0:2, 32 : 32 + thin] = gains[:, d * thin : (d + 1) * thin]
        tiles_ref[d, 0:1, 64 : 64 + part] = to_gain[:, d * part : (d + 1) * part]
        tiles_ref[d, 0:part, 96 : 96 + heads] = to_weight[d * part : (d + 1) * part, :]
    me = me_ref[0]
    step = len(outs)
    for m, out in enumerate(outs):
        for k in range(out.shape[0]):
            out[k] = tiles_ref[pl.ds(2 * (me ^ (k * step + m)), 2)]


def small_sums(me, crops, groups, *operands):
    step = 1 << groups[0]
    vm = pl.BlockSpec(memory_space=pltpu.VMEM)
    return pl.pallas_call(
        functools.partial(small_kernel, groups),
        in_specs=[pl.BlockSpec(memory_space=pltpu.SMEM)] + [vm] * len(operands),
        out_specs=[vm] * step,
        out_shape=[jax.ShapeDtypeStruct((crops // step, 2, 8, 128), F32)] * step,
        scratch_shapes=[pltpu.VMEM((2 * crops, 8, 128), F32)],
        cost_estimate=pl.CostEstimate(flops=0, transcendentals=0, bytes_accessed=4 << 20),
        name="small_sums",
    )(me, *operands)


def spread(parts, shift):
    count = lax.axis_size("crop")
    return [
        lax.ppermute(part, "crop", [(i, i ^ (m << shift)) for i in range(count)]) for m, part in enumerate(parts) if m
    ]


def flipped(index, mask):
    out, bit = index, 1
    while bit <= mask:
        if mask & bit:
            out = out + (1 - 2 * ((index // bit) % 2)) * bit
        bit *= 2
    return out


def small_tiles(tiles_ref, sums0_ref, sums1_ref, gain0_ref, gain1_ref, n_ref, c_ref, pair_gain_ref, pair_weight_ref):
    devices = tiles_ref.shape[0]
    heads, chan = n_ref.shape
    normed = n_ref[...] - jnp.sum(c_ref[...], axis=1, keepdims=True)
    to_weight = (normed * pair_gain_ref[...].astype(F32)).T
    to_gain = total(pair_weight_ref[...].astype(F32) * normed)
    biases = jnp.concatenate([sums0_ref[0:2, :], sums1_ref[...], sums0_ref[2:3, :]], axis=0)
    gains = jnp.concatenate([gain0_ref[...], gain1_ref[...]], axis=0)
    wide, thin, part = biases.shape[1] // devices, gains.shape[1] // devices, chan // devices
    for d in range(devices):
        tiles_ref[d] = jnp.zeros(tiles_ref.shape[1:], F32)
        tiles_ref[d, 0:5, 0:wide] = biases[:, d * wide : (d + 1) * wide]
        tiles_ref[d, 0:2, 32 : 32 + thin] = gains[:, d * thin : (d + 1) * thin]
        tiles_ref[d, 0:1, 64 : 64 + part] = to_gain[:, d * part : (d + 1) * part]
        tiles_ref[d, 0:part, 96 : 96 + heads] = to_weight[d * part : (d + 1) * part, :]


def finish_kernel(plan, orders, totals, sizes, *refs):
    tall, flat, long, small_at = sizes
    colors = len(orders)
    bits = len(orders[0])
    blocks = 1 << bits
    refs = list(refs)

    def take(count):
        out = refs[:count]
        del refs[:count]
        return out

    x_own_hbm, x_recv_hbm, g_own_hbm, g_send_hbm = take(4)
    small_refs = take(8)
    t_keep_a, t_keep_b, t_add_a, t_add_b = take(4)
    attn_ref, out_ref, cond_ref, small_ref, expand_ref, contract_ref = take(6)
    x_own, x_recv, g_own, g_recv, turned_ref, tiles_ref = take(6)
    parts = take(colors)
    landing = [take(bits) for _ in range(colors)]
    mine = take(colors)
    theirs = take(colors)
    t_mine, t_theirs = take(2), take(2)
    in_sems, send_sems, recv_sems = take(3)
    me = lax.axis_index("crop")
    side = lax.axis_index("seq")
    copies = fetch([(x_own_hbm, x_own), (x_recv_hbm, x_recv), (g_own_hbm, g_own)], in_sems)
    barrier = pltpu.get_barrier_semaphore()
    partners = [(flipped(me, 1 << bit), side) for bit in range(bits)] + [(me, 1 - side)]
    for partner in partners:
        pl.semaphore_signal(barrier, inc=1, device_id=partner, device_id_type=pl.DeviceIdType.MESH)
    pl.semaphore_wait(barrier, len(partners))
    used = [0]

    def ship(source, target, partner):
        k = used[0]
        used[0] += 1
        copy = pltpu.make_async_remote_copy(
            src_ref=source,
            dst_ref=target,
            send_sem=send_sems.at[k],
            recv_sem=recv_sems.at[k],
            device_id=partner,
            device_id_type=pl.DeviceIdType.MESH,
        )
        copy.start()
        return copy

    other_core = (me, 1 - side)
    across = ship(g_send_hbm, g_recv, other_core)
    for ref, keep, arrived in ((t_mine[0], t_keep_a, t_add_a), (t_mine[1], t_keep_b, t_add_b)):
        ref[...] = keep[0].astype(F32) + arrived[0].astype(F32)
    t_across = [ship(t_mine[k], t_theirs[k], other_core) for k in range(2)]
    small_tiles(tiles_ref, *small_refs)
    small_color, small_row = small_at
    for p in range(blocks):
        c = flipped(me, place(p, orders[small_color]))
        pair = tiles_ref[pl.ds(2 * c, 2)].astype(BF16)
        parts[small_color][p, small_row : small_row + 8, 0:128] = pair[0]
        parts[small_color][p, small_row : small_row + 8, 128:256] = pair[1]
        parts[small_color][p, small_row : small_row + 8, 256:384] = jnp.zeros((8, 128), BF16)
    copies[0].wait()
    copies[1].wait()

    flying = [[None] * bits for _ in range(colors)]

    def launch(color, j):
        count = blocks >> j
        bit = orders[color][j]
        partner = (flipped(me, 1 << bit), side)
        cuts = [(3 * count // 4, count), (count // 2, 3 * count // 4)] if count >= 4 else [(1, 2)]
        flying[color][j] = [
            (
                ship(
                    parts[color].at[low:high],
                    landing[color][j].at[low - count // 2 : high - count // 2],
                    partner,
                ),
                low - count // 2,
                high - count // 2,
            )
            for low, high in cuts
        ]

    last = [max(k for k, group in enumerate(plan) if any(use[1] == color for use in group[3])) for color in range(colors)]
    for k, (source, start, width, uses) in enumerate(plan):
        height = width // blocks
        if k == 0:
            copies[2].wait()
            across.wait()
        own, recv = ((x_own, x_recv), (g_own, g_recv))[source]
        span = slice(start, start + width)
        turned_ref[:width, :] = jnp.concatenate([own[:, span], recv[:, span]], axis=0).astype(F32).T
        for color in range(colors):
            wanted = [use for use in uses if use[1] == color]
            if wanted:
                left = jnp.concatenate(
                    [
                        turned_ref[pl.ds(flipped(me, place(p, orders[color])) * height, height), :]
                        for p in range(blocks)
                    ],
                    axis=0,
                ).astype(BF16)
            for column, _, offset in wanted:
                cut = slice(column, column + TILE)
                term = dot_nn(left, jnp.concatenate([g_own[:, cut], g_recv[:, cut]], axis=0)).astype(BF16)
                for p in range(blocks):
                    parts[color][p, offset : offset + height, :] = term[p * height : (p + 1) * height]
            if k == last[color]:
                launch(color, 0)

    def land(color, j, which):
        copy, low, high = flying[color][j][which]
        copy.wait()
        for p in range(low, high):
            both = parts[color][p].astype(F32) + landing[color][j][p].astype(F32)
            if j == bits - 1:
                mine[color][...] = both
            else:
                parts[color][p] = both.astype(BF16)

    for j in range(bits):
        for color in range(colors):
            land(color, j, 0)
            if j + 1 < bits:
                launch(color, j + 1)
        for color in range(colors):
            if len(flying[color][j]) > 1:
                land(color, j, 1)
        if j == 0:
            for copy in t_across:
                copy.wait()
            write_trans(tall, long, flat, side, t_mine, t_theirs, expand_ref, contract_ref, cond_ref)
    closing = [ship(mine[color], theirs[color], other_core) for color in range(colors)]
    for copy in closing:
        copy.wait()
    write_attn(tall, flat, side, mine, theirs, attn_ref, out_ref, cond_ref)
    ours = mine[small_color][small_row : small_row + 8, :]
    also = theirs[small_color][small_row : small_row + 8, :]
    both = ours + also
    small_ref[...] = jnp.where(side == 0, both[:, 0:128], both[:, 128:256])


def write_trans(tall, long, flat, side, mine, theirs, expand_ref, contract_ref, cond_ref):
    def unit(color, offset, height):
        return sides(side, mine[color], theirs[color], offset, height)

    for t in range(4):
        low, high = unit(0, t * tall, tall) if t < 3 else unit(1, 0, tall)
        expand_ref[:, 0, t * TILE : (t + 1) * TILE] = low
        expand_ref[:, 1, t * TILE : (t + 1) * TILE] = high
    low, high = unit(1, tall, long)
    contract_ref[:, :TILE] = low
    contract_ref[:, TILE:] = high
    low, high = unit(0, 3 * tall, flat)
    cond_ref[:, 3, :TILE] = low
    cond_ref[:, 4, :TILE] = high
    low, high = unit(1, tall + long, flat)
    cond_ref[:, 3, TILE:] = low
    cond_ref[:, 4, TILE:] = high
    low, high = unit(1, tall + long + flat, flat)
    cond_ref[:, 5, :TILE] = low
    cond_ref[:, 5, TILE:] = high


def write_attn(tall, flat, side, mine, theirs, attn_ref, out_ref, cond_ref):
    def unit(color, offset, height):
        return sides(side, mine[color], theirs[color], offset, height)

    spots = ((0, 0), (0, tall), (1, 0), (2, 0))
    for t, (color, offset) in enumerate(spots):
        low, high = unit(color, offset, tall)
        cut = slice((t % 2) * TILE, (t % 2 + 1) * TILE)
        attn_ref[:, t // 2, cut] = low
        attn_ref[:, 2 + t // 2, cut] = high
    low, high = unit(1, tall, tall)
    out_ref[:, :TILE] = low
    out_ref[:, TILE:] = high
    for t, (color, offset) in enumerate(((0, 2 * tall), (1, 2 * tall))):
        low, high = unit(color, offset, flat)
        cond_ref[:, 0, t * TILE : (t + 1) * TILE] = low
        cond_ref[:, 1, t * TILE : (t + 1) * TILE] = high
    low, high = unit(2, tall, flat)
    cond_ref[:, 2, :TILE] = low
    cond_ref[:, 2, TILE:] = high


def finish(crops, x_own, x_recv, g_own, g_send, small, state_t, arrived_t, sizes, first):
    tall, flat, long = sizes
    bits = crops.bit_length() - 1
    rows, width = x_own.shape[0], tall * crops
    cond_width, hidden_width = flat * crops, long * crops
    orders = (
        tuple(range(bits)),
        (1, 0) + tuple(range(2, bits)),
        tuple(range(2, bits)) + (0, 1),
    )
    c = [first + k * TILE for k in range(8)]
    plan = (
        (0, 0, width, ((c[0], 0, 0), (c[1], 0, tall), (c[2], 1, 0), (c[3], 2, 0))),
        (0, 2 * width, cond_width, ((c[5], 0, 2 * tall), (c[6], 1, 2 * tall))),
        (1, 0, width, ((c[4], 1, tall),)),
        (0, 2 * width + 2 * cond_width, cond_width, ((c[7], 2, tall),)),
    )
    totals = (2 * tall + flat, 2 * tall + flat + 8, tall + flat)
    small_at = (1, 2 * tall + flat)
    colors = len(orders)
    vm = pl.BlockSpec(memory_space=pltpu.VMEM)
    hbm = pl.BlockSpec(memory_space=pl.ANY)
    t_shapes = [keep.shape[1:] for keep, _ in state_t]
    ships = 1 + 2 + colors * (2 * (bits - 1) + 1) + colors
    devices = 2 * crops
    return pl.pallas_call(
        functools.partial(finish_kernel, plan, orders, totals, (tall, flat, long, small_at)),
        in_specs=[hbm] * 4 + [vm] * 12,
        out_specs=[vm] * 6,
        out_shape=[
            jax.ShapeDtypeStruct((tall // 2, 4, width), F32),
            jax.ShapeDtypeStruct((tall // 2, width), F32),
            jax.ShapeDtypeStruct((flat // 2, 6, width), F32),
            jax.ShapeDtypeStruct((8, 128), F32),
            jax.ShapeDtypeStruct((tall // 2, 2, hidden_width), F32),
            jax.ShapeDtypeStruct((long // 2, width), F32),
        ],
        scratch_shapes=[pltpu.VMEM(x_own.shape, BF16)] * 2
        + [pltpu.VMEM(g_own.shape, BF16)] * 2
        + [pltpu.VMEM((width, 2 * rows), F32), pltpu.VMEM((devices, 8, 128), F32)]
        + [pltpu.VMEM((crops, count, TILE), BF16) for count in totals]
        + [pltpu.VMEM((crops >> (j + 1), count, TILE), BF16) for count in totals for j in range(bits)]
        + [pltpu.VMEM((count, TILE), F32) for count in totals] * 2
        + [pltpu.VMEM(shape, F32) for shape in t_shapes] * 2
        + [
            pltpu.SemaphoreType.DMA((3,)),
            pltpu.SemaphoreType.DMA((ships,)),
            pltpu.SemaphoreType.DMA((ships,)),
        ],
        compiler_params=pltpu.CompilerParams(collective_id=1, has_side_effects=True),
        name="finish",
    )(
        x_own, x_recv, g_own, g_send, *small,
        state_t[0][0], state_t[1][0], arrived_t[0], arrived_t[1],
    )


def tie(*values):
    return lax.optimization_barrier(values)


def body(
    single,
    conditioning,
    pair_features,
    segments,
    pad_mask,
    cotangent,
    cond_gain,
    cond_weight,
    biases,
    attn_weight,
    out_weight,
    pair_gain,
    pair_weight,
    expand_weight,
    contract_weight,
):
    rows, width = single.shape
    cond_width = conditioning.shape[1]
    heads = pair_weight.shape[1]
    hidden_width = contract_weight.shape[0]
    crops = lax.axis_size("crop")
    bits = crops.bit_length() - 1
    me = lax.axis_index("crop").astype(jnp.int32).reshape(1)
    side = lax.axis_index("seq").astype(jnp.int32).reshape(1)
    orders = (tuple(range(bits)), (1, 0) + tuple(range(2, bits)))
    devices = 2 * crops
    chan_part = pair_gain.shape[0] // devices
    gains = cond_gain.T
    cond_weights = cond_weight.transpose(1, 0, 2)
    expand_weights = expand_weight.transpose(1, 0, 2)
    pair = pair_features[0]
    own_segments = lax.dynamic_slice(segments[0], (side[0] * rows,), (rows,))[:, None]

    x, scale0, keep0, own_t, send_t, kept, grad_norm1, grad_cond1, direct1, sums1, gain_sum1, w_forward, w_backward = trans(
        side, single, conditioning, cotangent, gains, biases.T, pair_gain[None], pair_weight.T,
        cond_weights, expand_weights, contract_weight,
    )
    x_other = swap(x)
    recv_t = swap(send_t)
    attn_weight, x = tie(attn_weight, x)
    attn_weights = attn_weight.transpose(1, 0, 2)
    attn_weights, x_other, recv_t = tie(attn_weights, x_other, recv_t)

    tall, flat, long = width // crops, cond_width // crops, hidden_width // crops
    low_at = 2 * width

    def columns(first):
        return [first + k * TILE for k in range(8)]

    c = columns(hidden_width)
    plan_t = (
        (0, width, width, ((c[0], 0, 0), (c[1], 0, tall), (c[2], 0, 2 * tall), (c[3], 1, 0))),
        (0, low_at + cond_width, cond_width, ((c[5], 0, 3 * tall), (c[6], 1, tall + long))),
        (1, 0, hidden_width, ((c[4], 1, tall),)),
        (0, low_at + 2 * cond_width, cond_width, ((c[7], 1, tall + long + flat),)),
    )
    totals_t = (3 * tall + flat, tall + long + 2 * flat)
    keep_a, send_a, keep_b, send_b = wgrad(me, x, x_other, own_t, recv_t, plan_t, orders, totals_t, "wgrad_trans")
    x, keep_a, send_a, keep_b, send_b = tie(x, keep_a, send_a, keep_b, send_b)
    state_t = [(keep_a, send_a), (keep_b, send_b)]
    arrived = arrivals(state_t, 0, orders)
    queries, kv, gate, grad_mixed, grad_attended = project(x, cotangent, biases.T, keep0, attn_weights, out_weight)
    kv_other = swap(kv)
    w_forward, grad_attended = tie(w_forward, grad_attended)
    bias, inv, mean = pair_fwd(pair, w_forward, heads)
    bias, kv_other, arrived = tie(bias, kv_other, arrived)
    state_t = added(state_t, arrived, "add_trans_0")
    bias, state_t = tie(bias, state_t)

    arrived = arrivals(state_t, 1, orders)
    attended, grad_queries, dkv_own, dkv_send, r, t, s = attention(
        side, queries, kv, kv_other, grad_attended, bias, inv, mean, own_segments, segments, pad_mask
    )
    dkv_send, arrived = tie(dkv_send, arrived)
    dkv_recv = swap(dkv_send)
    state_t = added(state_t, arrived, "add_trans_1")
    r, state_t = tie(r, state_t)

    arrived = arrivals(state_t, 2, orders)
    grad_pair, n_sum, c_sum = pair_bwd(pair, r, t, s, mean, w_backward)
    n_sum, dkv_recv, arrived = tie(n_sum, dkv_recv, arrived)
    state_t = added(state_t, arrived, "add_trans_2")
    dkv_recv, state_t = tie(dkv_recv, state_t)

    arrived = arrivals(state_t, 3, orders)
    own_a, sent_a, layer_out, grad_single, grad_cond, sums0, gain_sum0 = after(
        side, single, conditioning, cotangent, gains, attended, gate, out_weight, keep0, kept, grad_queries,
        dkv_own, dkv_recv, grad_mixed, attn_weights, scale0, cond_weights, grad_norm1, grad_cond1, direct1,
    )
    own_a, sent_a, arrived = tie(own_a, sent_a, arrived)
    for j in range(4, bits):
        state_t = added(state_t, arrived, "add_trans_" + str(j - 1))
        arrived = arrivals(state_t, j, orders)
    small_operands = (sums0, sums1, gain_sum0, gain_sum1, n_sum, c_sum, pair_gain[None], pair_weight.T)

    def results(attn, out, cond, small, expand, contract):
        return (
            layer_out,
            grad_single,
            grad_cond,
            grad_pair[None],
            small[:2, 32 : 32 + cond_width // devices].T,
            cond,
            small[:5, : width // devices].T,
            attn,
            out,
            small[0, 64 : 64 + chan_part],
            small[:chan_part, 96 : 96 + heads],
            expand,
            contract,
        )

    if tall % 8 == 0 and flat % 8 == 0:
        return results(
            *finish(crops, x, x_other, own_a, sent_a, small_operands, state_t, arrived, (tall, flat, long), width)
        )

    recv_a = swap(sent_a)
    c = columns(width)
    plan_a = (
        (0, 0, width, ((c[0], 0, 0), (c[1], 0, tall), (c[2], 0, 2 * tall), (c[3], 1, 0))),
        (1, 0, width, ((c[4], 1, tall),)),
        (0, low_at, cond_width, ((c[5], 1, 2 * tall), (c[6], 1, 2 * tall + flat))),
        (0, low_at + 2 * cond_width, cond_width, ((c[7], 1, 2 * tall + 2 * flat),)),
    )
    totals_a = (3 * tall, 2 * tall + 3 * flat)
    keep_a, send_a, keep_b, send_b = wgrad(me, x, x_other, own_a, recv_a, plan_a, orders, totals_a, "wgrad_attn")
    state_a = [(keep_a, send_a), (keep_b, send_b)]
    arrived_a = arrivals(state_a, 0, orders)
    state_t = added(state_t, arrived, "add_trans_last")
    trans_a, trans_b = state_t[0][0], state_t[1][0]
    trans_ra, trans_rb = swap(trans_a), swap(trans_b)
    state_a = added(state_a, arrived_a, "add_attn_0")
    arrived_a = arrivals(state_a, 1, orders)
    groups = tuple(min(2, bits - k) for k in range(0, bits, 2))
    parts = small_sums(me, crops, groups, *small_operands)
    landed = spread(parts, 0)
    trans_a, landed = tie(trans_a, landed)
    grad_expand, grad_contract, cond1 = close(
        functools.partial(close_trans_kernel, tall, long, flat),
        side,
        (trans_a, trans_b, trans_ra, trans_rb),
        ((tall // 2, 2, hidden_width), (long // 2, width), (3, flat // 2, width)),
        "close_trans",
    )
    shift = 0
    for j in range(1, bits):
        small_keep = parts[0]
        for v in landed:
            small_keep = small_keep + v
        cond1, small_keep, arrived_a = tie(cond1, small_keep, arrived_a)
        state_a = added(state_a, arrived_a, "add_attn_" + str(j))
        state_a, small_keep = tie(state_a, small_keep)
        if j + 1 < bits:
            arrived_a = arrivals(state_a, j + 1, orders)
        if j < len(groups):
            shift += groups[j - 1]
            step = 1 << groups[j]
            stacked = small_keep.reshape((-1, step) + small_keep.shape[1:])
            parts = [stacked[:, m] for m in range(step)]
            landed = spread(parts, shift)
        else:
            parts, landed = [small_keep], []
            if j == len(groups):
                small = small_keep[0]
                mine = jnp.where(side[0] == 0, small[0], small[1])
                small = mine + swap(jnp.where(side[0] == 0, small[1], small[0]))
                parts = [small]
    attn_a, attn_b = state_a[0][0], state_a[1][0]
    attn_ra, attn_rb = swap(attn_a), swap(attn_b)
    small = small_keep
    grad_attn_weight, grad_out, grad_cond_weight = close(
        functools.partial(close_attn_kernel, tall, flat),
        side,
        (attn_a, attn_b, attn_ra, attn_rb, cond1),
        ((tall // 2, 4, width), (tall // 2, width), (flat // 2, 6, width)),
        "close_attn",
    )
    return results(grad_attn_weight, grad_out, grad_cond_weight, small, grad_expand, grad_contract)


def solution(mesh):
    token = P(("crop", "seq"), None)
    whole = P()
    cube = P(("crop", "seq"), None, None)
    return jax.shard_map(
        body,
        mesh=mesh,
        in_specs=(token, token, P("crop", "seq", None, None), P("crop", None), P("crop", None), token)
        + (whole,) * 9,
        out_specs=(
            token, token, token, P("crop", "seq", None, None), token, cube, token, cube, token,
            P(("crop", "seq")), token, cube, token,
        ),
        check_vma=False,
    )
```

```python
import functools
import math
import jax
import jax.numpy as jnp
from jax import lax
from jax.experimental import pallas as pl
from jax.experimental.pallas import tpu as pltpu
from jax.sharding import PartitionSpec as P

EPS = 1e-05
NEG = -1e30
F32 = jnp.float32
BF16 = jnp.bfloat16


def dot_nt(a, b):
    return lax.dot_general(a, b, (((1,), (1,)), ((), ())), preferred_element_type=F32)


def dot_tn(a, b):
    return lax.dot_general(a, b, (((0,), (0,)), ((), ())), preferred_element_type=F32)


def dot_nn(a, b):
    return jnp.dot(a, b, preferred_element_type=F32)


def split3(v):
    hi = v.astype(BF16)
    rest = v - hi.astype(F32)
    mid = rest.astype(BF16)
    lo = (rest - mid.astype(F32)).astype(BF16)
    return hi, mid, lo


def pair_fwd_kernel(x_ref, w_ref, bias_ref, inv_ref, mean_ref):
    rows, keys, chan = x_ref.shape
    heads = bias_ref.shape[0]
    w = w_ref[...]
    ones = jnp.full((8, chan), 1.0, BF16)
    for base in range(0, rows, 8):
        parts = []
        invs = []
        means = []
        for i in range(base, base + 8):
            x = x_ref[i]
            raw = dot_nt(w, x)
            mean = raw[3 * heads : 3 * heads + 1] * (1.0 / chan)
            wide = x.astype(F32)
            centred = wide - jnp.mean(wide, axis=-1, keepdims=True)
            square = (centred * centred).astype(BF16)
            var = dot_nt(ones, square)[0:1] * (1.0 / chan)
            inv = lax.rsqrt(var + EPS)
            parts.append((raw[:heads] + raw[heads : 2 * heads] + raw[2 * heads : 3 * heads]) * inv)
            invs.append(inv)
            means.append(mean)
        block = jnp.stack(parts, axis=0)
        bias_ref[:, base : base + 8, :] = pltpu.einshape("ihj->hij", block).astype(BF16)
        inv_ref[base : base + 8, :] = jnp.concatenate(invs, axis=0)
        mean_ref[base : base + 8, :] = jnp.concatenate(means, axis=0)


def pair_fwd(x, w, heads, tile=32):
    rows, keys, chan = x.shape
    return pl.pallas_call(
        pair_fwd_kernel,
        grid=(rows // tile,),
        in_specs=[
            pl.BlockSpec((tile, keys, chan), lambda i: (i, 0, 0)),
            pl.BlockSpec(w.shape, lambda i: (0, 0)),
        ],
        out_specs=[
            pl.BlockSpec((heads, tile, keys), lambda i: (0, i, 0)),
            pl.BlockSpec((tile, keys), lambda i: (i, 0)),
            pl.BlockSpec((tile, keys), lambda i: (i, 0)),
        ],
        out_shape=[
            jax.ShapeDtypeStruct((heads, rows, keys), BF16),
            jax.ShapeDtypeStruct((rows, keys), F32),
            jax.ShapeDtypeStruct((rows, keys), F32),
        ],
        cost_estimate=pl.CostEstimate(flops=0, transcendentals=0, bytes_accessed=96 << 20),
        name="pair_fwd",
    )(x, w)


def attn_kernel(
    half_ref, q_ref, ko_ref, vo_ref, kr_ref, vr_ref, ga_ref, bias_ref, inv_ref, mean_ref, segc_ref, segr_ref, padr_ref,
    att_ref, dq_ref, own_ref, send_ref, r_ref, t_ref, s_ref,
    k_sc, v_sc, mask_sc, dk_sc, dv_sc, m2_sc,
):
    rows = q_ref.shape[0]
    heads, _, keys = bias_ref.shape
    size = q_ref.shape[1] // heads
    scale = 1.0 / math.sqrt(size)
    half = half_ref[0]
    own = pl.ds(pl.multiple_of(half * rows, 32), rows)
    other = pl.ds(pl.multiple_of((1 - half) * rows, 32), rows)
    k_sc[own, :] = ko_ref[...]
    k_sc[other, :] = kr_ref[...]
    v_sc[own, :] = vo_ref[...]
    v_sc[other, :] = vr_ref[...]

    @pl.when(pl.program_id(0) == 0)
    def _():
        row_id = lax.broadcasted_iota(jnp.int32, (rows, keys), 0) + half * rows
        col_id = lax.broadcasted_iota(jnp.int32, (rows, keys), 1)
        allowed = (segc_ref[...] == segr_ref[...]) & ((padr_ref[...] == 1) | (row_id == col_id))
        mask_sc[...] = jnp.where(allowed, 0.0, NEG)
        m2_sc[...] = jnp.zeros_like(m2_sc)

    inv = inv_ref[...]
    m2 = m2_sc[...]
    for h in range(heads):
        cut = slice(h * size, (h + 1) * size)
        qh = q_ref[:, cut]
        kh = k_sc[:, cut]
        vh = v_sc[:, cut]
        gh = ga_ref[:, cut]
        bias = bias_ref[h].astype(F32)
        scores = dot_nt(qh, kh) * scale + bias + mask_sc[...]
        top = jnp.max(scores, axis=-1, keepdims=True)
        e = jnp.exp(scores - top)
        p = e * (1.0 / jnp.sum(e, axis=-1, keepdims=True))
        low = p.astype(BF16)
        att_ref[:, cut] = dot_nn(low, vh).astype(BF16)
        gp = dot_nt(gh, vh)
        pg = p * gp
        delta = jnp.sum(pg, axis=-1, keepdims=True)
        gs32 = pg - p * delta
        gs = gs32.astype(BF16)
        dq_ref[:, cut] = (dot_nn(gs, kh) * scale).astype(BF16)
        dk_sc[:, cut] = dot_tn(gs, qh) * scale
        dv_sc[:, cut] = dot_tn(low, gh)
        m2 = m2 + gs32 * bias
        r_ref[h] = (gs.astype(F32) * inv).astype(BF16)
    m2_sc[...] = m2
    own_ref[0] = dk_sc[own, :]
    own_ref[1] = dv_sc[own, :]
    send_ref[0] = dk_sc[other, :]
    send_ref[1] = dv_sc[other, :]

    @pl.when(pl.program_id(0) == pl.num_programs(0) - 1)
    def _():
        slope = inv * inv * m2 * (1.0 / 128.0)
        s_ref[...] = -slope
        t_ref[...] = slope * mean_ref[...]


def attention(half, q, kv, kv_other, ga, bias, inv, mean, segc, segr, padr):
    rows, width = q.shape
    heads, _, keys = bias.shape
    groups = 2
    part = width // groups

    def lanes(first):
        return pl.BlockSpec((rows, part), lambda g: (0, first + g))

    def fixed(shape):
        return pl.BlockSpec(shape, lambda g: (0,) * len(shape))

    plane = fixed((rows, keys))
    pair = pl.BlockSpec((2, rows, part), lambda g: (0, 0, g))
    head = pl.BlockSpec((heads // groups, rows, keys), lambda g: (g, 0, 0))
    return pl.pallas_call(
        attn_kernel,
        grid=(groups,),
        in_specs=[
            pl.BlockSpec(memory_space=pltpu.SMEM),
            lanes(0), lanes(0), lanes(groups), lanes(0), lanes(groups), lanes(0), head, plane, plane,
            fixed(segc.shape), fixed(segr.shape), fixed(padr.shape),
        ],
        out_specs=[lanes(0), lanes(0), pair, pair, head, plane, plane],
        out_shape=[
            jax.ShapeDtypeStruct((rows, width), BF16),
            jax.ShapeDtypeStruct((rows, width), BF16),
            jax.ShapeDtypeStruct((2, rows, width), F32),
            jax.ShapeDtypeStruct((2, rows, width), F32),
            jax.ShapeDtypeStruct((heads, rows, keys), BF16),
            jax.ShapeDtypeStruct((rows, keys), F32),
            jax.ShapeDtypeStruct((rows, keys), F32),
        ],
        scratch_shapes=[
            pltpu.VMEM((keys, part), BF16),
            pltpu.VMEM((keys, part), BF16),
            pltpu.VMEM((rows, keys), F32),
            pltpu.VMEM((keys, part), F32),
            pltpu.VMEM((keys, part), F32),
            pltpu.VMEM((rows, keys), F32),
        ],
        cost_estimate=pl.CostEstimate(flops=0, transcendentals=0, bytes_accessed=60 << 20),
        name="attn",
    )(half, q, kv, kv, kv_other, kv_other, ga, bias, inv, mean, segc, segr, padr)


def pair_bwd_kernel(x_ref, r_ref, t_ref, s_ref, mean_ref, w_ref, out_ref, n_ref, c_ref):
    rows, keys, chan = x_ref.shape
    heads = r_ref.shape[0]
    depth = w_ref.shape[0]
    w = w_ref[...]

    @pl.when(pl.program_id(0) == 0)
    def _():
        n_ref[...] = jnp.zeros_like(n_ref)
        c_ref[...] = jnp.zeros_like(c_ref)

    acc = jnp.zeros(n_ref.shape, F32)
    corr = jnp.zeros(c_ref.shape, F32)
    pad = jnp.zeros((depth - 2 * heads - 6, keys), F32)
    for base in range(0, rows, 8):
        block = pltpu.einshape("hij->ihj", r_ref[:, base : base + 8, :].astype(F32))
        for k in range(8):
            i = base + k
            r32 = block[k]
            t = t_ref[i : i + 1, :]
            s = s_ref[i : i + 1, :]
            th, tm, tl = (v.astype(F32) for v in split3(t))
            sh, sm, sl = (v.astype(F32) for v in split3(s))
            left = jnp.concatenate([r32, r32, th, tm, tl, sh, sm, sl, pad], axis=0).astype(BF16)
            both = dot_tn(left, w)
            x = x_ref[i]
            out_ref[i] = (both[:, :chan] + x.astype(F32) * both[:, chan:]).astype(BF16)
            acc = acc + dot_nn(r32.astype(BF16), x)
            corr = corr + r32 * mean_ref[i : i + 1, :]
    n_ref[...] += acc
    c_ref[...] += corr


def pair_bwd(x, r, t, s, mean, w, tile=32):
    rows, keys, chan = x.shape
    heads = r.shape[0]
    return pl.pallas_call(
        pair_bwd_kernel,
        grid=(rows // tile,),
        in_specs=[
            pl.BlockSpec((tile, keys, chan), lambda i: (i, 0, 0)),
            pl.BlockSpec((heads, tile, keys), lambda i: (0, i, 0)),
            pl.BlockSpec((tile, keys), lambda i: (i, 0)),
            pl.BlockSpec((tile, keys), lambda i: (i, 0)),
            pl.BlockSpec((tile, keys), lambda i: (i, 0)),
            pl.BlockSpec(w.shape, lambda i: (0, 0)),
        ],
        out_specs=[
            pl.BlockSpec((tile, keys, chan), lambda i: (i, 0, 0)),
            pl.BlockSpec((heads, chan), lambda i: (0, 0)),
            pl.BlockSpec((heads, keys), lambda i: (0, 0)),
        ],
        out_shape=[
            jax.ShapeDtypeStruct((rows, keys, chan), BF16),
            jax.ShapeDtypeStruct((heads, chan), F32),
            jax.ShapeDtypeStruct((heads, keys), F32),
        ],
        cost_estimate=pl.CostEstimate(flops=0, transcendentals=0, bytes_accessed=60 << 20),
        name="pair_bwd",
    )(x, r, t, s, mean, w)


def norm_rows(values):
    centred = values - jnp.mean(values, -1, keepdims=True)
    inverse = lax.rsqrt(jnp.mean(centred * centred, -1, keepdims=True) + EPS)
    return (centred * inverse, inverse)


def norm_back(incoming, normal, inverse):
    return inverse * (
        incoming
        - jnp.mean(incoming, -1, keepdims=True)
        - normal * jnp.mean(incoming * normal, -1, keepdims=True)
    )


def sigmoid(v):
    return jax.nn.sigmoid(v)


def fetch(pairs, sems):
    copies = [pltpu.make_async_copy(src, dst, sems.at[k]) for k, (src, dst) in enumerate(pairs)]
    for copy in copies:
        copy.start()
    return copies


def put(side, own_ref, send_ref, start, low, high):
    stop = start + low.shape[1]

    @pl.when(side == 0)
    def _():
        own_ref[:, start:stop] = low
        send_ref[:, start:stop] = high

    @pl.when(side != 0)
    def _():
        own_ref[:, start:stop] = high
        send_ref[:, start:stop] = low


def total(v):
    return jnp.sum(v.astype(F32), axis=0, keepdims=True)


def pair_weights(gain_ref, weight_ref, forward_ref, backward_ref):
    gained = weight_ref[...].astype(F32) * gain_ref[...].astype(F32)
    heads, chan = gained.shape
    hi, mid, lo = split3(gained - jnp.mean(gained, axis=1, keepdims=True))
    forward_ref[0:heads, :] = hi
    forward_ref[heads : 2 * heads, :] = mid
    forward_ref[2 * heads : 3 * heads, :] = lo
    row = lax.broadcasted_iota(jnp.int32, (16, chan), 0)
    forward_ref[3 * heads :, :] = jnp.where(row == 0, 1.0, 0.0).astype(BF16)
    backward_ref[0:heads, :chan] = hi
    backward_ref[heads : 2 * heads, :chan] = mid
    backward_ref[0 : 2 * heads, chan:] = jnp.zeros((2 * heads, chan), BF16)
    backward_ref[2 * heads :, :chan] = jnp.where(row < 3, 1.0, 0.0).astype(BF16)
    backward_ref[2 * heads :, chan:] = jnp.where((row >= 3) & (row < 6), 1.0, 0.0).astype(BF16)


def trans_kernel(
    side_ref, single_ref, cond_ref, cot_ref, gain_ref, bias_ref, pair_gain_ref, pair_weight_ref, cw_hbm, ew_hbm, tw_hbm,
    x_hbm, scale0_hbm, keep0_hbm,
    own_ref, send_ref, kept_ref, grad_norm_ref, grad_cond_ref, grad_direct_ref, sums_ref, gain_sum_ref,
    forward_ref, backward_ref,
    cw, ew, tw, x_ref, scale0_ref, keep0_ref, scale1_ref, sems, out_sems,
):
    order = (3, 4, 5, 0, 1, 2)
    copies = fetch(
        [(cw_hbm.at[k], cw.at[k]) for k in order[:3]]
        + [(ew_hbm.at[0], ew.at[0]), (ew_hbm.at[1], ew.at[1]), (tw_hbm, tw)]
        + [(cw_hbm.at[k], cw.at[k]) for k in order[3:]],
        sems,
    )
    side = side_ref[0]
    rows, width = single_ref.shape
    cond_width = cond_ref.shape[1]
    cut = width // 2
    hidden_width = tw.shape[0]
    pair_weights(pair_gain_ref, pair_weight_ref, forward_ref, backward_ref)
    single_norm, _ = norm_rows(single_ref[...].astype(F32))
    cond_norm, _ = norm_rows(cond_ref[...].astype(F32))
    cond = cond_ref[...]
    x_ref[:, 2 * width + 2 * cond_width :] = cond

    def modulate(b, waits, scale_ref):
        low = (cond_norm * gain_ref[b : b + 1, :].astype(F32)).astype(BF16)
        x_ref[:, 2 * width + b * cond_width : 2 * width + (b + 1) * cond_width] = low
        waits[0].wait()
        scale = sigmoid(dot_nn(low, cw[3 * b]) + bias_ref[2 * b : 2 * b + 1, :].astype(F32))
        scale_ref[...] = scale
        waits[1].wait()
        shift = dot_nn(low, cw[3 * b + 1])
        x_ref[:, b * width : (b + 1) * width] = (scale * single_norm + shift).astype(BF16)
        waits[2].wait()
        return sigmoid(dot_nn(cond, cw[3 * b + 2]) + bias_ref[2 * b + 1 : 2 * b + 2, :].astype(F32))

    keep = modulate(1, copies[:3], scale1_ref)
    keep0_ref[...] = modulate(0, copies[6:], scale0_ref)
    leaving = fetch([(x_ref, x_hbm), (scale0_ref, scale0_hbm), (keep0_ref, keep0_hbm)], out_sems)
    trans_in = x_ref[:, width : 2 * width]
    upstream = cot_ref[...].astype(F32)
    grad_trans = (upstream * keep).astype(BF16)
    at = hidden_width
    put(side, own_ref, send_ref, at + hidden_width, grad_trans[:, :cut], grad_trans[:, cut:])
    for copy in copies[3:6]:
        copy.wait()
    grad_in = jnp.zeros((rows, width), F32)
    trans_out = jnp.zeros((rows, width), F32)
    step = 512
    for c in range(0, hidden_width, step):
        span = slice(c, c + step)
        gate_pre = dot_nn(trans_in, ew[0, :, span])
        up_pre = dot_nn(trans_in, ew[1, :, span])
        sig = sigmoid(gate_pre)
        act = gate_pre * sig
        hidden = (act * up_pre).astype(BF16)
        own_ref[:, span] = hidden
        send_ref[:, span] = hidden
        trans_out = trans_out + dot_nn(hidden, tw[span, :])
        grad_hidden = dot_nt(grad_trans, tw[span, :])
        grad_gate = (grad_hidden * up_pre * sig * (1.0 + gate_pre * (1.0 - sig))).astype(BF16)
        grad_up = (grad_hidden * act).astype(BF16)
        put(side, own_ref, send_ref, at + c, grad_gate, grad_up)
        grad_in = grad_in + dot_nt(grad_gate, ew[0, :, span]) + dot_nt(grad_up, ew[1, :, span])
    kept_ref[...] = keep * trans_out
    grad_keep = (upstream * trans_out * keep * (1.0 - keep)).astype(BF16)
    finish_branch(
        side, 1, 2 * hidden_width + cut, (), cw.at[3:6], single_ref, cond_ref, gain_ref, scale1_ref, grad_in, grad_keep,
        own_ref, send_ref, grad_norm_ref, grad_cond_ref, grad_direct_ref, sums_ref, gain_sum_ref,
    )
    for copy in leaving:
        copy.wait()


def trans(side, single, cond, cot, gains, biases, pair_gain, pair_weight, cw, ew, tw):
    rows, width = single.shape
    cond_width = cond.shape[1]
    hidden_width = tw.shape[0]
    heads, chan = pair_weight.shape
    packed = 2 * hidden_width + width // 2 + width + width // 2
    x_width = 2 * width + 3 * cond_width
    vm = pl.BlockSpec(memory_space=pltpu.VMEM)
    hbm = pl.BlockSpec(memory_space=pl.ANY)
    wide = jax.ShapeDtypeStruct((rows, width), F32)
    narrow = jax.ShapeDtypeStruct((rows, cond_width), F32)
    return pl.pallas_call(
        trans_kernel,
        in_specs=[pl.BlockSpec(memory_space=pltpu.SMEM)] + [vm] * 7 + [hbm] * 3,
        out_specs=[hbm] * 3 + [vm] * 10,
        out_shape=[
            jax.ShapeDtypeStruct((rows, x_width), BF16),
            wide,
            wide,
            jax.ShapeDtypeStruct((rows, packed), BF16),
            jax.ShapeDtypeStruct((rows, packed), BF16),
            wide,
            wide,
            narrow,
            narrow,
            jax.ShapeDtypeStruct((2, width), F32),
            jax.ShapeDtypeStruct((1, cond_width), F32),
            jax.ShapeDtypeStruct((3 * heads + 16, chan), BF16),
            jax.ShapeDtypeStruct((2 * heads + 16, 2 * chan), BF16),
        ],
        scratch_shapes=[
            pltpu.VMEM(cw.shape, BF16),
            pltpu.VMEM(ew.shape, BF16),
            pltpu.VMEM(tw.shape, BF16),
            pltpu.VMEM((rows, x_width), BF16),
            pltpu.VMEM((rows, width), F32),
            pltpu.VMEM((rows, width), F32),
            pltpu.VMEM((rows, width), F32),
            pltpu.SemaphoreType.DMA((9,)),
            pltpu.SemaphoreType.DMA((3,)),
        ],
        cost_estimate=pl.CostEstimate(flops=0, transcendentals=0, bytes_accessed=50 << 20),
        name="trans",
    )(side, single, cond, cot, gains, biases, pair_gain, pair_weight, cw, ew, tw)


def finish_branch(
    side, b, at, copies, cw, single_ref, cond_ref, gain_ref, scale_ref, grad_in, grad_keep,
    own_ref, send_ref, grad_norm_ref, grad_cond_ref, grad_direct_ref, sums_ref, gain_sum_ref,
):
    width = single_ref.shape[1]
    cut = width // 2
    single_norm, _ = norm_rows(single_ref[...].astype(F32))
    cond_norm, _ = norm_rows(cond_ref[...].astype(F32))
    scale = scale_ref[...]
    grad_scale = (grad_in * single_norm * scale * (1.0 - scale)).astype(BF16)
    grad_shift = grad_in.astype(BF16)
    put(side, own_ref, send_ref, at, grad_scale, grad_shift)
    put(side, own_ref, send_ref, at + width, grad_keep[:, :cut], grad_keep[:, cut:])
    grad_norm_ref[...] = grad_in * scale
    for copy in copies:
        copy.wait()
    grad_low = dot_nt(grad_scale, cw[0]) + dot_nt(grad_shift, cw[1])
    grad_cond_ref[...] = grad_low * gain_ref[b : b + 1, :].astype(F32)
    grad_direct_ref[...] = dot_nt(grad_keep, cw[2])
    gain_sum_ref[...] = total(grad_low * cond_norm)
    sums_ref[0:1, :] = total(grad_scale)
    sums_ref[1:2, :] = total(grad_keep)


def project_kernel(
    x_hbm, cot_ref, bias_ref, keep_hbm, aw_hbm, ow_hbm, q_ref, kv_ref, gate_ref, mixed_ref, attended_ref,
    x, keep, aw, ow, sems,
):
    width = cot_ref.shape[1]
    copies = fetch(
        [(x_hbm.at[:, :width], x)] + [(aw_hbm.at[k], aw.at[k]) for k in range(4)] + [(keep_hbm, keep), (ow_hbm, ow)], sems
    )
    copies[0].wait()
    copies[1].wait()
    q_ref[...] = (dot_nn(x[...], aw[0]) + bias_ref[4:5, :].astype(F32)).astype(BF16)
    copies[2].wait()
    kv_ref[:, :width] = dot_nn(x[...], aw[1]).astype(BF16)
    copies[3].wait()
    kv_ref[:, width:] = dot_nn(x[...], aw[2]).astype(BF16)
    copies[4].wait()
    gate = sigmoid(dot_nn(x[...], aw[3]))
    gate_ref[...] = gate
    copies[5].wait()
    grad_attn = (cot_ref[...].astype(F32) * keep[...]).astype(BF16)
    copies[6].wait()
    grad_mixed = dot_nt(grad_attn, ow[...])
    mixed_ref[...] = grad_mixed
    attended_ref[...] = (grad_mixed * gate).astype(BF16)


def project(x, cot, biases, keep, aw, ow):
    rows, width = cot.shape
    vm = pl.BlockSpec(memory_space=pltpu.VMEM)
    hbm = pl.BlockSpec(memory_space=pl.ANY)
    return pl.pallas_call(
        project_kernel,
        in_specs=[hbm, vm, vm, hbm, hbm, hbm],
        out_specs=[vm] * 5,
        out_shape=[
            jax.ShapeDtypeStruct((rows, width), BF16),
            jax.ShapeDtypeStruct((rows, 2 * width), BF16),
            jax.ShapeDtypeStruct((rows, width), F32),
            jax.ShapeDtypeStruct((rows, width), F32),
            jax.ShapeDtypeStruct((rows, width), BF16),
        ],
        scratch_shapes=[
            pltpu.VMEM((rows, width), BF16),
            pltpu.VMEM((rows, width), F32),
            pltpu.VMEM(aw.shape, BF16),
            pltpu.VMEM(ow.shape, BF16),
            pltpu.SemaphoreType.DMA((7,)),
        ],
        cost_estimate=pl.CostEstimate(flops=0, transcendentals=0, bytes_accessed=22 << 20),
        name="project",
    )(x, cot, biases, keep, aw, ow)


def after_kernel(
    side_ref, single_ref, cond_ref, cot_ref, gain_ref,
    attended_hbm, gate_hbm, ow_hbm, keep_hbm, kept_hbm, grad_q_hbm, dkv_own_hbm, dkv_recv_hbm, grad_mixed_hbm, aw_hbm,
    scale_hbm, cw_hbm, grad_norm1_hbm, grad_cond1_hbm, direct1_hbm,
    own_ref, send_ref, layer_hbm, grad_single_ref, grad_cond_ref, sums_ref, gain_sum_ref,
    attended_ref, gate_ref, ow, keep_ref, kept_ref, grad_q_ref, dkv_own_ref, dkv_recv_ref, grad_mixed_ref, aw,
    scale_ref, cw, grad_norm1_ref, grad_cond1_ref, direct1_ref, layer_ref, norm_sc, cond_sc, direct_sc, sems, out_sem,
):
    sources = [
        (attended_hbm, attended_ref), (gate_hbm, gate_ref), (ow_hbm, ow), (keep_hbm, keep_ref), (kept_hbm, kept_ref),
        (grad_q_hbm, grad_q_ref), (dkv_own_hbm, dkv_own_ref), (dkv_recv_hbm, dkv_recv_ref),
        (grad_mixed_hbm, grad_mixed_ref),
    ]
    sources += [(aw_hbm.at[k], aw.at[k]) for k in range(4)]
    sources += [(scale_hbm, scale_ref)] + [(cw_hbm.at[k], cw.at[k]) for k in range(3)]
    sources += [(grad_norm1_hbm, grad_norm1_ref), (grad_cond1_hbm, grad_cond1_ref), (direct1_hbm, direct1_ref)]
    copies = fetch(sources, sems)
    side = side_ref[0]
    width = single_ref.shape[1]
    cut = width // 2
    upstream = cot_ref[...].astype(F32)
    single_norm, single_inverse = norm_rows(single_ref[...].astype(F32))
    cond_norm, cond_inverse = norm_rows(cond_ref[...].astype(F32))
    copies[0].wait()
    copies[1].wait()
    gate = gate_ref[...]
    attended = attended_ref[...].astype(F32)
    mixed = (attended * gate).astype(BF16)
    own_ref[:, :width] = mixed
    send_ref[:, :width] = mixed
    copies[2].wait()
    attn_out = dot_nn(mixed, ow[...])
    copies[3].wait()
    keep = keep_ref[...]
    copies[4].wait()
    layer_ref[...] = (single_ref[...].astype(F32) + keep * attn_out + kept_ref[...]).astype(BF16)
    leaving = pltpu.make_async_copy(layer_ref, layer_hbm, out_sem)
    leaving.start()
    grad_keep = (upstream * attn_out * keep * (1.0 - keep)).astype(BF16)
    grad_attn = (upstream * keep).astype(BF16)
    put(side, own_ref, send_ref, 3 * width, grad_attn[:, :cut], grad_attn[:, cut:])
    for copy in copies[5:9]:
        copy.wait()
    grad_q = grad_q_ref[...]
    grad_k = (dkv_own_ref[0] + dkv_recv_ref[0]).astype(BF16)
    grad_v = (dkv_own_ref[1] + dkv_recv_ref[1]).astype(BF16)
    grad_logit = (grad_mixed_ref[...] * attended * gate * (1.0 - gate)).astype(BF16)
    put(side, own_ref, send_ref, width, grad_q, grad_v)
    put(side, own_ref, send_ref, 2 * width, grad_k, grad_logit)
    sums_ref[2:3, :] = total(grad_q)
    grad_in = jnp.zeros(single_ref.shape, F32)
    for k, part in enumerate((grad_q, grad_k, grad_v, grad_logit)):
        copies[9 + k].wait()
        grad_in = grad_in + dot_nt(part, aw[k])
    copies[13].wait()
    finish_branch(
        side, 0, 3 * width + cut, copies[14:17], cw, single_ref, cond_ref, gain_ref, scale_ref, grad_in, grad_keep,
        own_ref, send_ref, norm_sc, cond_sc, direct_sc, sums_ref, gain_sum_ref,
    )
    for copy in copies[17:]:
        copy.wait()
    grad_single_ref[...] = upstream + norm_back(norm_sc[...] + grad_norm1_ref[...], single_norm, single_inverse)
    grad_cond_ref[...] = (
        norm_back(cond_sc[...] + grad_cond1_ref[...], cond_norm, cond_inverse) + (direct_sc[...] + direct1_ref[...])
    )
    leaving.wait()


def after(side, single, cond, cot, gains, attended, gate, ow, keep, kept, grad_q, dkv_own, dkv_recv, grad_mixed, aw,
          scale, cw, grad_norm1, grad_cond1, direct1):
    rows, width = single.shape
    cond_width = cond.shape[1]
    packed = 3 * width + width // 2 + width + width // 2
    vm = pl.BlockSpec(memory_space=pltpu.VMEM)
    hbm = pl.BlockSpec(memory_space=pl.ANY)
    moved = (attended, gate, ow, keep, kept, grad_q, dkv_own, dkv_recv, grad_mixed, aw, scale, cw,
             grad_norm1, grad_cond1, direct1)
    shapes = [(3,) + v.shape[1:] if v is cw else v.shape for v in moved]
    return pl.pallas_call(
        after_kernel,
        in_specs=[pl.BlockSpec(memory_space=pltpu.SMEM)] + [vm] * 4 + [hbm] * len(moved),
        out_specs=[vm, vm, hbm] + [vm] * 4,
        out_shape=[
            jax.ShapeDtypeStruct((rows, packed), BF16),
            jax.ShapeDtypeStruct((rows, packed), BF16),
            jax.ShapeDtypeStruct((rows, width), BF16),
            jax.ShapeDtypeStruct((rows, width), F32),
            jax.ShapeDtypeStruct((rows, cond_width), F32),
            jax.ShapeDtypeStruct((3, width), F32),
            jax.ShapeDtypeStruct((1, cond_width), F32),
        ],
        scratch_shapes=[pltpu.VMEM(shape, v.dtype) for shape, v in zip(shapes, moved)]
        + [
            pltpu.VMEM((rows, width), BF16),
            pltpu.VMEM((rows, width), F32),
            pltpu.VMEM((rows, cond_width), F32),
            pltpu.VMEM((rows, cond_width), F32),
            pltpu.SemaphoreType.DMA((20,)),
            pltpu.SemaphoreType.DMA,
        ],
        cost_estimate=pl.CostEstimate(flops=0, transcendentals=0, bytes_accessed=40 << 20),
        name="after",
    )(side, single, cond, cot, gains, *moved)


TILE = 384


def place(position, order):
    count = len(order)
    return sum(((position >> (count - 1 - j)) & 1) << order[j] for j in range(count))


def wgrad_kernel(plan, orders, me_ref, *refs):
    sources, outs = refs[:4], refs[4:8]
    (x_own, x_recv, g_own, g_recv), turned_ref, results, sems, out_sems = refs[8:12], refs[12], refs[13:17], refs[17], refs[18]
    copies = fetch(list(zip(sources, (x_own, x_recv, g_own, g_recv))), sems)
    copies[0].wait()
    copies[1].wait()
    me = me_ref[0]
    blocks = 1 << len(orders[0])
    last = [max(k for k, group in enumerate(plan) if any(use[1] == color for use in group[3])) for color in (0, 1)]
    leaving = []
    for k, (source, start, width, uses) in enumerate(plan):
        height = width // blocks
        own, recv = ((x_own, x_recv), (g_own, g_recv))[source]
        span = slice(start, start + width)
        turned_ref[:width, :] = jnp.concatenate([own[:, span], recv[:, span]], axis=0).astype(F32).T
        if k == 0:
            copies[2].wait()
            copies[3].wait()
        for color in (0, 1):
            mine = [use for use in uses if use[1] == color]
            if mine:
                left = jnp.concatenate(
                    [
                        turned_ref[pl.ds(pl.multiple_of((me ^ place(p, orders[color])) * height, 8), height), :]
                        for p in range(blocks)
                    ],
                    axis=0,
                ).astype(BF16)
            keep_ref, send_ref = results[2 * color], results[2 * color + 1]
            for column, _, offset in mine:
                cut = slice(column, column + TILE)
                term = dot_nn(left, jnp.concatenate([g_own[:, cut], g_recv[:, cut]], axis=0)).astype(BF16)
                for p in range(blocks):
                    target = keep_ref if p < blocks // 2 else send_ref
                    target[p % (blocks // 2), offset : offset + height, :] = term[p * height : (p + 1) * height]
            if k == last[color]:
                for j in (2 * color, 2 * color + 1):
                    copy = pltpu.make_async_copy(results[j], outs[j], out_sems.at[j])
                    copy.start()
                    leaving.append(copy)
    for copy in leaving:
        copy.wait()


def wgrad(me, x_own, x_recv, g_own, g_recv, plan, orders, totals, name):
    rows = x_own.shape[0]
    blocks = 1 << len(orders[0])
    half = blocks // 2
    if any((width // blocks) % 8 for _, _, width, _ in plan):
        return wgrad_plain(me, x_own, x_recv, g_own, g_recv, plan, orders, totals)
    hbm = pl.BlockSpec(memory_space=pl.ANY)
    shapes = [(half, count, TILE) for count in totals for _ in range(2)]
    widest = max(group[2] for group in plan)
    moved = (x_own, x_recv, g_own, g_recv)
    return pl.pallas_call(
        functools.partial(wgrad_kernel, plan, orders),
        in_specs=[pl.BlockSpec(memory_space=pltpu.SMEM)] + [hbm] * 4,
        out_specs=[hbm] * 4,
        out_shape=[jax.ShapeDtypeStruct(shape, BF16) for shape in shapes],
        scratch_shapes=[pltpu.VMEM(v.shape, v.dtype) for v in moved]
        + [pltpu.VMEM((widest, 2 * rows), F32)]
        + [pltpu.VMEM(shape, BF16) for shape in shapes]
        + [pltpu.SemaphoreType.DMA((4,)), pltpu.SemaphoreType.DMA((4,))],
        cost_estimate=pl.CostEstimate(flops=0, transcendentals=0, bytes_accessed=26 << 20),
        name=name,
    )(me, *moved)


def wgrad_plain(me, x_own, x_recv, g_own, g_recv, plan, orders, totals):
    blocks = 1 << len(orders[0])
    pieces = ([], [])
    for source, start, width, uses in plan:
        own, recv = ((x_own, x_recv), (g_own, g_recv))[source]
        x = jnp.concatenate([own[:, start : start + width], recv[:, start : start + width]], axis=0)
        for column, color, offset in uses:
            g = jnp.concatenate([g_own[:, column : column + TILE], g_recv[:, column : column + TILE]], axis=0)
            wanted = jnp.stack([me[0] ^ place(p, orders[color]) for p in range(blocks)])
            term = jnp.take(dot_tn(x, g).reshape(blocks, width // blocks, TILE), wanted, axis=0)
            pieces[color].append((offset, term.astype(BF16)))
    outs = []
    for parts in pieces:
        whole = jnp.concatenate([term for _, term in sorted(parts, key=lambda part: part[0])], axis=1)
        outs += [whole[: blocks // 2], whole[blocks // 2 :]]
    return outs


def send_half(value, bit):
    count = lax.axis_size("crop")
    return lax.ppermute(value, "crop", [(i, i ^ (1 << bit)) for i in range(count)])


def arrivals(state, j, orders):
    return [send_half(send, order[j]) for (_, send), order in zip(state, orders)]


def add_kernel(*refs):
    if refs[0].shape[0] == 1 and len(refs) == 6:
        for color in (0, 1):
            refs[4 + color][...] = refs[2 * color][0].astype(F32) + refs[2 * color + 1][0].astype(F32)
        return
    for color in (0, 1):
        low, high, other_low, other_high = refs[4 * color : 4 * color + 4]
        keep, send = refs[8 + 2 * color : 10 + 2 * color]
        keep[...] = (low[...].astype(F32) + other_low[...].astype(F32)).astype(BF16)
        send[...] = (high[...].astype(F32) + other_high[...].astype(F32)).astype(BF16)


def added(state, arrived, name):
    count = state[0][0].shape[0]
    half = count // 2
    operands, in_specs, out_specs, out_shape = [], [], [], []
    for (keep, _), other in zip(state, arrived):
        block = (1,) + keep.shape[1:]
        if half:
            low = pl.BlockSpec(block, lambda p: (p, 0, 0))
            high = pl.BlockSpec(block, lambda p: (p + half, 0, 0))
            operands += [keep, keep, other, other]
            in_specs += [low, high, low, high]
            out_specs += [low, low]
            out_shape += [jax.ShapeDtypeStruct((half,) + keep.shape[1:], BF16)] * 2
        else:
            operands += [keep, other]
            in_specs += [pl.BlockSpec(memory_space=pltpu.VMEM)] * 2
            out_specs += [pl.BlockSpec(memory_space=pltpu.VMEM)]
            out_shape += [jax.ShapeDtypeStruct(keep.shape[1:], F32)]
    out = pl.pallas_call(
        add_kernel,
        grid=(half,) if half else (),
        in_specs=in_specs,
        out_specs=out_specs,
        out_shape=out_shape,
        cost_estimate=pl.CostEstimate(flops=0, transcendentals=0, bytes_accessed=2 << 20),
        name=name,
    )(*operands)
    return [(out[0], out[1]), (out[2], out[3])] if half else [(v, None) for v in out]


def swap(v):
    return lax.ppermute(v, "seq", [(0, 1), (1, 0)])


def rows_of(side, ref, offset, height):
    v = ref[offset : offset + height, :]
    return jnp.where(side == 0, v[: height // 2], v[height // 2 :])


def sides(side, mine_ref, recv_ref, offset, height):
    mine = rows_of(side, mine_ref, offset, height)
    recv = rows_of(side, recv_ref, offset, height)
    return jnp.where(side == 0, mine, recv), jnp.where(side == 0, recv, mine)


def close_trans_kernel(tall, long, flat, side_ref, a_ref, b_ref, ra_ref, rb_ref, expand_ref, contract_ref, cond_ref):
    side = side_ref[0]
    for t in range(4):
        refs = (a_ref, ra_ref, t * tall) if t < 3 else (b_ref, rb_ref, 0)
        low, high = sides(side, *refs, tall)
        expand_ref[:, 0, t * TILE : (t + 1) * TILE] = low
        expand_ref[:, 1, t * TILE : (t + 1) * TILE] = high
    low, high = sides(side, b_ref, rb_ref, tall, long)
    contract_ref[:, :TILE] = low
    contract_ref[:, TILE:] = high
    low, high = sides(side, a_ref, ra_ref, 3 * tall, flat)
    cond_ref[0, :, :TILE] = low
    cond_ref[1, :, :TILE] = high
    low, high = sides(side, b_ref, rb_ref, tall + long, flat)
    cond_ref[0, :, TILE:] = low
    cond_ref[1, :, TILE:] = high
    low, high = sides(side, b_ref, rb_ref, tall + long + flat, flat)
    cond_ref[2, :, :TILE] = low
    cond_ref[2, :, TILE:] = high


def close_attn_kernel(tall, flat, side_ref, a_ref, b_ref, ra_ref, rb_ref, cond_in, attn_ref, out_ref, cond_ref):
    side = side_ref[0]
    for t in range(4):
        refs = (a_ref, ra_ref, t * tall) if t < 3 else (b_ref, rb_ref, 0)
        low, high = sides(side, *refs, tall)
        cut = slice((t % 2) * TILE, (t % 2 + 1) * TILE)
        attn_ref[:, t // 2, cut] = low
        attn_ref[:, 2 + t // 2, cut] = high
    low, high = sides(side, b_ref, rb_ref, tall, tall)
    out_ref[:, :TILE] = low
    out_ref[:, TILE:] = high
    for t in range(2):
        low, high = sides(side, b_ref, rb_ref, 2 * tall + t * flat, flat)
        cond_ref[:, 0, t * TILE : (t + 1) * TILE] = low
        cond_ref[:, 1, t * TILE : (t + 1) * TILE] = high
    low, high = sides(side, b_ref, rb_ref, 2 * tall + 2 * flat, flat)
    cond_ref[:, 2, :TILE] = low
    cond_ref[:, 2, TILE:] = high
    for k in range(3):
        cond_ref[:, 3 + k, :] = cond_in[k]


def close(kernel, side, operands, shapes, name):
    vm = pl.BlockSpec(memory_space=pltpu.VMEM)
    return pl.pallas_call(
        kernel,
        in_specs=[pl.BlockSpec(memory_space=pltpu.SMEM)] + [vm] * len(operands),
        out_specs=[vm] * len(shapes),
        out_shape=[jax.ShapeDtypeStruct(shape, F32) for shape in shapes],
        cost_estimate=pl.CostEstimate(flops=0, transcendentals=0, bytes_accessed=4 << 20),
        name=name,
    )(side, *operands)


def small_kernel(
    groups, me_ref, sums0_ref, sums1_ref, gain0_ref, gain1_ref, n_ref, c_ref, pair_gain_ref, pair_weight_ref, *refs
):
    outs, tiles_ref = refs[:-1], refs[-1]
    devices = tiles_ref.shape[0]
    heads, chan = n_ref.shape
    normed = n_ref[...] - jnp.sum(c_ref[...], axis=1, keepdims=True)
    to_weight = (normed * pair_gain_ref[...].astype(F32)).T
    to_gain = total(pair_weight_ref[...].astype(F32) * normed)
    biases = jnp.concatenate([sums0_ref[0:2, :], sums1_ref[...], sums0_ref[2:3, :]], axis=0)
    gains = jnp.concatenate([gain0_ref[...], gain1_ref[...]], axis=0)
    wide, thin, part = biases.shape[1] // devices, gains.shape[1] // devices, chan // devices
    for d in range(devices):
        tiles_ref[d] = jnp.zeros(tiles_ref.shape[1:], F32)
        tiles_ref[d, 0:5, 0:wide] = biases[:, d * wide : (d + 1) * wide]
        tiles_ref[d, 0:2, 32 : 32 + thin] = gains[:, d * thin : (d + 1) * thin]
        tiles_ref[d, 0:1, 64 : 64 + part] = to_gain[:, d * part : (d + 1) * part]
        tiles_ref[d, 0:part, 96 : 96 + heads] = to_weight[d * part : (d + 1) * part, :]
    me = me_ref[0]
    step = len(outs)
    for m, out in enumerate(outs):
        for k in range(out.shape[0]):
            out[k] = tiles_ref[pl.ds(2 * (me ^ (k * step + m)), 2)]


def small_sums(me, crops, groups, *operands):
    step = 1 << groups[0]
    vm = pl.BlockSpec(memory_space=pltpu.VMEM)
    return pl.pallas_call(
        functools.partial(small_kernel, groups),
        in_specs=[pl.BlockSpec(memory_space=pltpu.SMEM)] + [vm] * len(operands),
        out_specs=[vm] * step,
        out_shape=[jax.ShapeDtypeStruct((crops // step, 2, 8, 128), F32)] * step,
        scratch_shapes=[pltpu.VMEM((2 * crops, 8, 128), F32)],
        cost_estimate=pl.CostEstimate(flops=0, transcendentals=0, bytes_accessed=4 << 20),
        name="small_sums",
    )(me, *operands)


def spread(parts, shift):
    count = lax.axis_size("crop")
    return [
        lax.ppermute(part, "crop", [(i, i ^ (m << shift)) for i in range(count)]) for m, part in enumerate(parts) if m
    ]


def flipped(index, mask):
    out, bit = index, 1
    while bit <= mask:
        if mask & bit:
            out = out + (1 - 2 * ((index // bit) % 2)) * bit
        bit *= 2
    return out


def small_tiles(tiles_ref, sums0_ref, sums1_ref, gain0_ref, gain1_ref, n_ref, c_ref, pair_gain_ref, pair_weight_ref):
    devices = tiles_ref.shape[0]
    heads, chan = n_ref.shape
    normed = n_ref[...] - jnp.sum(c_ref[...], axis=1, keepdims=True)
    to_weight = (normed * pair_gain_ref[...].astype(F32)).T
    to_gain = total(pair_weight_ref[...].astype(F32) * normed)
    biases = jnp.concatenate([sums0_ref[0:2, :], sums1_ref[...], sums0_ref[2:3, :]], axis=0)
    gains = jnp.concatenate([gain0_ref[...], gain1_ref[...]], axis=0)
    wide, thin, part = biases.shape[1] // devices, gains.shape[1] // devices, chan // devices
    for d in range(devices):
        tiles_ref[d] = jnp.zeros(tiles_ref.shape[1:], F32)
        tiles_ref[d, 0:5, 0:wide] = biases[:, d * wide : (d + 1) * wide]
        tiles_ref[d, 0:2, 32 : 32 + thin] = gains[:, d * thin : (d + 1) * thin]
        tiles_ref[d, 0:1, 64 : 64 + part] = to_gain[:, d * part : (d + 1) * part]
        tiles_ref[d, 0:part, 96 : 96 + heads] = to_weight[d * part : (d + 1) * part, :]


def finish_kernel(plan, orders, small_at, *refs):
    small_color, small_row = small_at
    colors = len(orders)
    bits = len(orders[0])
    blocks = 1 << bits
    refs = list(refs)

    def take(count):
        out = refs[:count]
        del refs[:count]
        return out

    x_own_hbm, x_recv_hbm, g_own_hbm, g_send_hbm = take(4)
    small_refs = take(8)
    t_keep_a, t_keep_b, t_add_a, t_add_b = take(4)
    mine, theirs = take(colors), take(colors)
    t_mine, t_theirs = take(2), take(2)
    x_own, x_recv, g_own, g_recv, turned_ref, tiles_ref = take(6)
    parts = take(colors)
    landing = [take(bits) for _ in range(colors)]
    in_sems, send_sems, recv_sems = take(3)
    me = lax.axis_index("crop")
    side = lax.axis_index("seq")
    copies = fetch([(x_own_hbm, x_own), (x_recv_hbm, x_recv), (g_own_hbm, g_own)], in_sems)
    barrier = pltpu.get_barrier_semaphore()
    partners = [(flipped(me, 1 << bit), side) for bit in range(bits)] + [(me, 1 - side)]
    for partner in partners:
        pl.semaphore_signal(barrier, inc=1, device_id=partner, device_id_type=pl.DeviceIdType.MESH)
    pl.semaphore_wait(barrier, len(partners))
    used = [0]

    def ship(source, target, partner):
        k = used[0]
        used[0] += 1
        copy = pltpu.make_async_remote_copy(
            src_ref=source,
            dst_ref=target,
            send_sem=send_sems.at[k],
            recv_sem=recv_sems.at[k],
            device_id=partner,
            device_id_type=pl.DeviceIdType.MESH,
        )
        copy.start()
        return copy

    other_core = (me, 1 - side)
    across = ship(g_send_hbm, g_recv, other_core)
    for ref, keep, arrived in ((t_mine[0], t_keep_a, t_add_a), (t_mine[1], t_keep_b, t_add_b)):
        ref[...] = keep[0].astype(F32) + arrived[0].astype(F32)
    t_across = [ship(t_mine[k], t_theirs[k], other_core) for k in range(2)]
    small_tiles(tiles_ref, *small_refs)
    for p in range(blocks):
        c = flipped(me, place(p, orders[small_color]))
        pair = tiles_ref[pl.ds(2 * c, 2)].astype(BF16)
        parts[small_color][p, small_row : small_row + 8, 0:128] = pair[0]
        parts[small_color][p, small_row : small_row + 8, 128:256] = pair[1]
        parts[small_color][p, small_row : small_row + 8, 256:384] = jnp.zeros((8, 128), BF16)
    copies[0].wait()
    copies[1].wait()

    flying = [[None] * bits for _ in range(colors)]

    def launch(color, j):
        count = blocks >> j
        bit = orders[color][j]
        partner = (flipped(me, 1 << bit), side)
        cuts = [(3 * count // 4, count), (count // 2, 3 * count // 4)] if count >= 4 else [(1, 2)]
        flying[color][j] = [
            (
                ship(
                    parts[color].at[low:high],
                    landing[color][j].at[low - count // 2 : high - count // 2],
                    partner,
                ),
                low - count // 2,
                high - count // 2,
            )
            for low, high in cuts
        ]

    last = [max(k for k, group in enumerate(plan) if any(use[1] == color for use in group[3])) for color in range(colors)]
    for k, (source, start, width, uses) in enumerate(plan):
        height = width // blocks
        if k == 0:
            copies[2].wait()
            across.wait()
        own, recv = ((x_own, x_recv), (g_own, g_recv))[source]
        span = slice(start, start + width)
        turned_ref[:width, :] = jnp.concatenate([own[:, span], recv[:, span]], axis=0).astype(F32).T
        for color in range(colors):
            wanted = [use for use in uses if use[1] == color]
            if wanted:
                left = jnp.concatenate(
                    [
                        turned_ref[pl.ds(flipped(me, place(p, orders[color])) * height, height), :]
                        for p in range(blocks)
                    ],
                    axis=0,
                ).astype(BF16)
            for column, _, offset in wanted:
                cut = slice(column, column + TILE)
                term = dot_nn(left, jnp.concatenate([g_own[:, cut], g_recv[:, cut]], axis=0)).astype(BF16)
                for p in range(blocks):
                    parts[color][p, offset : offset + height, :] = term[p * height : (p + 1) * height]
            if k == last[color]:
                launch(color, 0)

    def land(color, j, which):
        copy, low, high = flying[color][j][which]
        copy.wait()
        for p in range(low, high):
            both = parts[color][p].astype(F32) + landing[color][j][p].astype(F32)
            if j == bits - 1:
                mine[color][...] = both
            else:
                parts[color][p] = both.astype(BF16)

    for j in range(bits):
        for color in range(colors):
            land(color, j, 0)
            if j + 1 < bits:
                launch(color, j + 1)
        for color in range(colors):
            if len(flying[color][j]) > 1:
                land(color, j, 1)
    closing = [ship(mine[color], theirs[color], other_core) for color in range(colors)]
    for copy in t_across + closing:
        copy.wait()


def write_trans(tall, long, flat, side, mine, theirs, expand_ref, contract_ref, cond_ref):
    def unit(color, offset, height):
        return sides(side, mine[color], theirs[color], offset, height)

    for t in range(4):
        low, high = unit(0, t * tall, tall) if t < 3 else unit(1, 0, tall)
        expand_ref[:, 0, t * TILE : (t + 1) * TILE] = low
        expand_ref[:, 1, t * TILE : (t + 1) * TILE] = high
    low, high = unit(1, tall, long)
    contract_ref[:, :TILE] = low
    contract_ref[:, TILE:] = high
    low, high = unit(0, 3 * tall, flat)
    cond_ref[:, 3, :TILE] = low
    cond_ref[:, 4, :TILE] = high
    low, high = unit(1, tall + long, flat)
    cond_ref[:, 3, TILE:] = low
    cond_ref[:, 4, TILE:] = high
    low, high = unit(1, tall + long + flat, flat)
    cond_ref[:, 5, :TILE] = low
    cond_ref[:, 5, TILE:] = high


def write_attn(tall, flat, side, mine, theirs, attn_ref, out_ref, cond_ref):
    def unit(color, offset, height):
        return sides(side, mine[color], theirs[color], offset, height)

    spots = ((0, 0), (0, tall), (1, 0), (2, 0))
    for t, (color, offset) in enumerate(spots):
        low, high = unit(color, offset, tall)
        cut = slice((t % 2) * TILE, (t % 2 + 1) * TILE)
        attn_ref[:, t // 2, cut] = low
        attn_ref[:, 2 + t // 2, cut] = high
    low, high = unit(1, tall, tall)
    out_ref[:, :TILE] = low
    out_ref[:, TILE:] = high
    for t, (color, offset) in enumerate(((0, 2 * tall), (1, 2 * tall))):
        low, high = unit(color, offset, flat)
        cond_ref[:, 0, t * TILE : (t + 1) * TILE] = low
        cond_ref[:, 1, t * TILE : (t + 1) * TILE] = high
    low, high = unit(2, tall, flat)
    cond_ref[:, 2, :TILE] = low
    cond_ref[:, 2, TILE:] = high


def outputs_kernel(sizes, *refs):
    tall, flat, long, small_at, heads = sizes
    side_ref, m0, m1, m2, h0, h1, h2, tm0, tm1, th0, th1 = refs[:11]
    attn_ref, out_ref, cond_ref, gain_ref, bias_ref, pair_gain_ref, pair_weight_ref, expand_ref, contract_ref = refs[11:]
    side = side_ref[0]
    mine, theirs = (m0, m1, m2), (h0, h1, h2)
    write_trans(tall, long, flat, side, (tm0, tm1), (th0, th1), expand_ref, contract_ref, cond_ref)
    write_attn(tall, flat, side, mine, theirs, attn_ref, out_ref, cond_ref)
    color, row = small_at
    both = mine[color][row : row + 8, :] + theirs[color][row : row + 8, :]
    small = jnp.where(side == 0, both[:, 0:128], both[:, 128:256])
    bias_ref[...] = small[:5, 0 : bias_ref.shape[1]]
    gain_ref[...] = small[:2, 32 : 32 + gain_ref.shape[1]]
    pair_gain_ref[...] = small[:1, 64 : 64 + pair_gain_ref.shape[1]]
    pair_weight_ref[...] = small[: pair_weight_ref.shape[0], 96 : 96 + heads]


def finish(crops, side, x_own, x_recv, g_own, g_send, small, state_t, arrived_t, sizes, first, heads, chan_part):
    tall, flat, long = sizes
    bits = crops.bit_length() - 1
    rows, width = x_own.shape[0], tall * crops
    cond_width, hidden_width = flat * crops, long * crops
    orders = (
        tuple(range(bits)),
        (1, 0) + tuple(range(2, bits)),
        tuple(range(2, bits)) + (0, 1),
    )
    c = [first + k * TILE for k in range(8)]
    plan = (
        (0, 0, width, ((c[0], 0, 0), (c[1], 0, tall), (c[2], 1, 0), (c[3], 2, 0))),
        (0, 2 * width, cond_width, ((c[5], 0, 2 * tall), (c[6], 1, 2 * tall))),
        (1, 0, width, ((c[4], 1, tall),)),
        (0, 2 * width + 2 * cond_width, cond_width, ((c[7], 2, tall),)),
    )
    totals = (2 * tall + flat, 2 * tall + flat + 8, tall + flat)
    small_at = (1, 2 * tall + flat)
    colors = len(orders)
    vm = pl.BlockSpec(memory_space=pltpu.VMEM)
    hbm = pl.BlockSpec(memory_space=pl.ANY)
    t_shapes = [keep.shape[1:] for keep, _ in state_t]
    shapes = [(count, TILE) for count in totals] * 2 + t_shapes * 2
    ships = 1 + 2 + colors * (2 * (bits - 1) + 1) + colors
    devices = 2 * crops
    sums = pl.pallas_call(
        functools.partial(finish_kernel, plan, orders, small_at),
        in_specs=[hbm] * 4 + [vm] * 12,
        out_specs=[vm] * len(shapes),
        out_shape=[jax.ShapeDtypeStruct(shape, F32) for shape in shapes],
        scratch_shapes=[pltpu.VMEM(x_own.shape, BF16)] * 2
        + [pltpu.VMEM(g_own.shape, BF16)] * 2
        + [pltpu.VMEM((width, 2 * rows), F32), pltpu.VMEM((devices, 8, 128), F32)]
        + [pltpu.VMEM((crops, count, TILE), BF16) for count in totals]
        + [pltpu.VMEM((crops >> (j + 1), count, TILE), BF16) for count in totals for j in range(bits)]
        + [
            pltpu.SemaphoreType.DMA((3,)),
            pltpu.SemaphoreType.DMA((ships,)),
            pltpu.SemaphoreType.DMA((ships,)),
        ],
        compiler_params=pltpu.CompilerParams(collective_id=1, has_side_effects=True),
        name="finish",
    )(
        x_own, x_recv, g_own, g_send, *small,
        state_t[0][0], state_t[1][0], arrived_t[0], arrived_t[1],
    )
    return close(
        functools.partial(outputs_kernel, (tall, flat, long, small_at, heads)),
        side,
        sums,
        (
            (tall // 2, 4, width), (tall // 2, width), (flat // 2, 6, width),
            (2, cond_width // devices), (5, width // devices), (1, chan_part), (chan_part, heads),
            (tall // 2, 2, hidden_width), (long // 2, width),
        ),
        "outputs",
    )


def tie(*values):
    return lax.optimization_barrier(values)


def body(
    single,
    conditioning,
    pair_features,
    segments,
    pad_mask,
    cotangent,
    cond_gain,
    cond_weight,
    biases,
    attn_weight,
    out_weight,
    pair_gain,
    pair_weight,
    expand_weight,
    contract_weight,
):
    rows, width = single.shape
    cond_width = conditioning.shape[1]
    heads = pair_weight.shape[1]
    hidden_width = contract_weight.shape[0]
    crops = lax.axis_size("crop")
    bits = crops.bit_length() - 1
    me = lax.axis_index("crop").astype(jnp.int32).reshape(1)
    side = lax.axis_index("seq").astype(jnp.int32).reshape(1)
    orders = (tuple(range(bits)), (1, 0) + tuple(range(2, bits)))
    devices = 2 * crops
    chan_part = pair_gain.shape[0] // devices
    gains = cond_gain.T
    cond_weights = cond_weight.transpose(1, 0, 2)
    expand_weights = expand_weight.transpose(1, 0, 2)
    pair = pair_features[0]
    own_segments = lax.dynamic_slice(segments[0], (side[0] * rows,), (rows,))[:, None]

    x, scale0, keep0, own_t, send_t, kept, grad_norm1, grad_cond1, direct1, sums1, gain_sum1, w_forward, w_backward = trans(
        side, single, conditioning, cotangent, gains, biases.T, pair_gain[None], pair_weight.T,
        cond_weights, expand_weights, contract_weight,
    )
    x_other = swap(x)
    recv_t = swap(send_t)
    attn_weight, x = tie(attn_weight, x)
    attn_weights = attn_weight.transpose(1, 0, 2)
    attn_weights, x_other, recv_t = tie(attn_weights, x_other, recv_t)

    tall, flat, long = width // crops, cond_width // crops, hidden_width // crops
    low_at = 2 * width

    def columns(first):
        return [first + k * TILE for k in range(8)]

    c = columns(hidden_width)
    plan_t = (
        (0, width, width, ((c[0], 0, 0), (c[1], 0, tall), (c[2], 0, 2 * tall), (c[3], 1, 0))),
        (0, low_at + cond_width, cond_width, ((c[5], 0, 3 * tall), (c[6], 1, tall + long))),
        (1, 0, hidden_width, ((c[4], 1, tall),)),
        (0, low_at + 2 * cond_width, cond_width, ((c[7], 1, tall + long + flat),)),
    )
    totals_t = (3 * tall + flat, tall + long + 2 * flat)
    keep_a, send_a, keep_b, send_b = wgrad(me, x, x_other, own_t, recv_t, plan_t, orders, totals_t, "wgrad_trans")
    x, keep_a, send_a, keep_b, send_b = tie(x, keep_a, send_a, keep_b, send_b)
    state_t = [(keep_a, send_a), (keep_b, send_b)]
    arrived = arrivals(state_t, 0, orders)
    queries, kv, gate, grad_mixed, grad_attended = project(x, cotangent, biases.T, keep0, attn_weights, out_weight)
    kv_other = swap(kv)
    w_forward, grad_attended = tie(w_forward, grad_attended)
    bias, inv, mean = pair_fwd(pair, w_forward, heads)
    bias, kv_other, arrived = tie(bias, kv_other, arrived)
    state_t = added(state_t, arrived, "add_trans_0")
    bias, state_t = tie(bias, state_t)

    arrived = arrivals(state_t, 1, orders)
    attended, grad_queries, dkv_own, dkv_send, r, t, s = attention(
        side, queries, kv, kv_other, grad_attended, bias, inv, mean, own_segments, segments, pad_mask
    )
    dkv_send, arrived = tie(dkv_send, arrived)
    dkv_recv = swap(dkv_send)
    state_t = added(state_t, arrived, "add_trans_1")
    r, state_t = tie(r, state_t)

    arrived = arrivals(state_t, 2, orders)
    grad_pair, n_sum, c_sum = pair_bwd(pair, r, t, s, mean, w_backward)
    n_sum, dkv_recv, arrived = tie(n_sum, dkv_recv, arrived)
    state_t = added(state_t, arrived, "add_trans_2")
    dkv_recv, state_t = tie(dkv_recv, state_t)

    arrived = arrivals(state_t, 3, orders)
    own_a, sent_a, layer_out, grad_single, grad_cond, sums0, gain_sum0 = after(
        side, single, conditioning, cotangent, gains, attended, gate, out_weight, keep0, kept, grad_queries,
        dkv_own, dkv_recv, grad_mixed, attn_weights, scale0, cond_weights, grad_norm1, grad_cond1, direct1,
    )
    own_a, sent_a, arrived = tie(own_a, sent_a, arrived)
    for j in range(4, bits):
        state_t = added(state_t, arrived, "add_trans_" + str(j - 1))
        arrived = arrivals(state_t, j, orders)
    small_operands = (sums0, sums1, gain_sum0, gain_sum1, n_sum, c_sum, pair_gain[None], pair_weight.T)

    def results(attn, out, cond, gain, bias, to_gain, to_weight, expand, contract):
        return (
            layer_out, grad_single, grad_cond, grad_pair[None], gain.T, cond, bias.T, attn, out,
            to_gain.reshape(-1), to_weight, expand, contract,
        )

    if tall % 8 == 0 and flat % 8 == 0:
        return results(
            *finish(
                crops, side, x, x_other, own_a, sent_a, small_operands, state_t, arrived, (tall, flat, long), width,
                heads, chan_part,
            )
        )

    recv_a = swap(sent_a)
    c = columns(width)
    plan_a = (
        (0, 0, width, ((c[0], 0, 0), (c[1], 0, tall), (c[2], 0, 2 * tall), (c[3], 1, 0))),
        (1, 0, width, ((c[4], 1, tall),)),
        (0, low_at, cond_width, ((c[5], 1, 2 * tall), (c[6], 1, 2 * tall + flat))),
        (0, low_at + 2 * cond_width, cond_width, ((c[7], 1, 2 * tall + 2 * flat),)),
    )
    totals_a = (3 * tall, 2 * tall + 3 * flat)
    keep_a, send_a, keep_b, send_b = wgrad(me, x, x_other, own_a, recv_a, plan_a, orders, totals_a, "wgrad_attn")
    state_a = [(keep_a, send_a), (keep_b, send_b)]
    arrived_a = arrivals(state_a, 0, orders)
    state_t = added(state_t, arrived, "add_trans_last")
    trans_a, trans_b = state_t[0][0], state_t[1][0]
    trans_ra, trans_rb = swap(trans_a), swap(trans_b)
    state_a = added(state_a, arrived_a, "add_attn_0")
    arrived_a = arrivals(state_a, 1, orders)
    groups = tuple(min(2, bits - k) for k in range(0, bits, 2))
    parts = small_sums(me, crops, groups, *small_operands)
    landed = spread(parts, 0)
    trans_a, landed = tie(trans_a, landed)
    grad_expand, grad_contract, cond1 = close(
        functools.partial(close_trans_kernel, tall, long, flat),
        side,
        (trans_a, trans_b, trans_ra, trans_rb),
        ((tall // 2, 2, hidden_width), (long // 2, width), (3, flat // 2, width)),
        "close_trans",
    )
    shift = 0
    for j in range(1, bits):
        small_keep = parts[0]
        for v in landed:
            small_keep = small_keep + v
        cond1, small_keep, arrived_a = tie(cond1, small_keep, arrived_a)
        state_a = added(state_a, arrived_a, "add_attn_" + str(j))
        state_a, small_keep = tie(state_a, small_keep)
        if j + 1 < bits:
            arrived_a = arrivals(state_a, j + 1, orders)
        if j < len(groups):
            shift += groups[j - 1]
            step = 1 << groups[j]
            stacked = small_keep.reshape((-1, step) + small_keep.shape[1:])
            parts = [stacked[:, m] for m in range(step)]
            landed = spread(parts, shift)
        else:
            parts, landed = [small_keep], []
            if j == len(groups):
                small = small_keep[0]
                mine = jnp.where(side[0] == 0, small[0], small[1])
                small = mine + swap(jnp.where(side[0] == 0, small[1], small[0]))
                parts = [small]
    attn_a, attn_b = state_a[0][0], state_a[1][0]
    attn_ra, attn_rb = swap(attn_a), swap(attn_b)
    small = small_keep
    grad_attn_weight, grad_out, grad_cond_weight = close(
        functools.partial(close_attn_kernel, tall, flat),
        side,
        (attn_a, attn_b, attn_ra, attn_rb, cond1),
        ((tall // 2, 4, width), (tall // 2, width), (flat // 2, 6, width)),
        "close_attn",
    )
    return results(
        grad_attn_weight, grad_out, grad_cond_weight, small[:2, 32 : 32 + cond_width // devices],
        small[:5, : width // devices], small[0, 64 : 64 + chan_part], small[:chan_part, 96 : 96 + heads],
        grad_expand, grad_contract,
    )


def solution(mesh):
    token = P(("crop", "seq"), None)
    whole = P()
    cube = P(("crop", "seq"), None, None)
    return jax.shard_map(
        body,
        mesh=mesh,
        in_specs=(token, token, P("crop", "seq", None, None), P("crop", None), P("crop", None), token)
        + (whole,) * 9,
        out_specs=(
            token, token, token, P("crop", "seq", None, None), token, cube, token, cube, token,
            P(("crop", "seq")), token, cube, token,
        ),
        check_vma=False,
    )
```
